256 devices in a mesh: strip: 128 (over x, y_hi, z, core), harm: 2 (over y_lo).
Axes of the slice: x: 4, y: 4 (y_hi: 2, y_lo: 2; y = y_hi * 2 + y_lo), z: 8, core: 2. Of those that a mesh axis runs over, the one named last changes fastest.
Arguments:
- edge_map: float32 [128, 256, 256], P('strip'), may hold values from -1 to 2
- couple_map: float32 [128, 256, 256], P('strip'), may hold values from -0.1 to 0.1
- topo_rows: float32 [128, 256, 256], P('strip'), may hold values from -0.375 to 0.375
- mass: float32 [128, 256], P('strip'), may hold values from 0.001 to 0.01
- col_blocks: int32 [128, 2], P('strip'), may hold values from 0 to 7, all different within a row
- gravity: float32 [1024, 1024], P('strip', 'harm'), may hold values from -0.5 to 10, as said below
Outputs:
- sensitivity: float32 [128, 256, 1024], P('strip', None, 'harm')
- factor: float32 [1024, 1024], P('strip', 'harm')
The draws below stay inside these ranges and needn't reach their ends.
Inputs may be any that keep to these rules, and one draw needn't show every extreme that they name: `col_blocks`: each row names 2 different blocks; every block is named by some strip. `gravity`: symmetric positive definite.
All inputs are finite; a program needn't handle non-finite values.
Results may differ from the reference program's by a relative error of at most 0.0003.
Values sent between devices are 32-bit elements; how exact they have to be, the bound alone decides.
A program may use at most 64 MiB of HBM per device.

```python
import math
import jax
import jax.numpy as jnp
from jax import lax

UNKNOWNS = 256
HARMONICS = 1024
COUPLED = 256
LEVELS = 2
COL_BLOCKS = 2
STRIPS = 128


def draw_edge_map(key, part):
    noise = jnp.clip(jax.random.normal(key, (STRIPS, UNKNOWNS, UNKNOWNS), jnp.float32), -6.0, 6.0)
    return jnp.eye(UNKNOWNS, dtype=jnp.float32) + 0.5 * noise / math.sqrt(UNKNOWNS)


def draw_couple_map(key, part):
    noise = jnp.clip(jax.random.normal(key, (STRIPS, UNKNOWNS, UNKNOWNS), jnp.float32), -6.0, 6.0)
    return 0.05 * noise / math.sqrt(UNKNOWNS)


def draw_gravity(key, part):
    base = jnp.clip(jax.random.normal(key, (HARMONICS, HARMONICS), jnp.float32), -6.0, 6.0)
    scales = jax.random.uniform(jax.random.fold_in(key, 3), (HARMONICS,), jnp.float32, 1.0, 4.0)
    gram = jnp.dot(base.T, base, precision=lax.Precision.HIGHEST) / HARMONICS
    return gram + jnp.diag(scales)


def steps_of(key, dims, split, low, largest):
    def one(position, blocks):
        steps = jax.random.uniform(jax.random.fold_in(jax.random.fold_in(key, 6), position), (blocks,), jnp.float32, low / len(split), largest / len(split))
        return jnp.repeat(jnp.exp(steps), dims[position] // blocks).reshape((-1,) + (1,) * (len(dims) - position - 1))

    level = one(*split[0])
    for cut in split[1:]:
        level = level * one(*cut)
    return level


def different_ones(stream_key, rows, count, top, lift):
    order = jax.random.permutation(jax.random.fold_in(stream_key, 1), count)
    favour = order
    for power in range(3):
        favour = favour * favour // count
    favour = favour * lift // count
    lots = jax.random.randint(jax.random.fold_in(stream_key, 2), (rows, count), 0, 4096) + favour
    sure = jax.random.permutation(jax.random.fold_in(stream_key, 3), rows)[jnp.arange(count) % rows]
    lots = jnp.where(jnp.arange(rows)[:, None] == sure[None, :], 1 << 14, lots)
    priority = lots * count + jnp.arange(count)
    return lax.top_k(priority.astype(jnp.int32), top)[1].astype(jnp.int32)


def bell_draw(own_key, shape, scale, reach, split=(), kind=jnp.bfloat16):
    array = jax.random.normal(own_key, shape, jnp.float32) * scale
    if len(split) > 0:
        array = steps_of(own_key, shape, split, -0.22, 0.18) * array
    return jnp.clip(array, min=-reach, max=reach).astype(kind)


def setup_inputs(seed: int = 0) -> dict:
    arg_keys = jax.random.split(jax.random.key(seed), 7)
    return {
        "edge_map": draw_edge_map(jax.random.fold_in(arg_keys[6], 71), 0),
        "couple_map": draw_couple_map(jax.random.fold_in(arg_keys[6], 71), 0),
        "topo_rows": bell_draw(arg_keys[2], (STRIPS, UNKNOWNS, COUPLED), UNKNOWNS ** -0.5, 0.375, ((0, 128),), jnp.float32),
        "mass": jnp.clip(jnp.exp(math.log(0.01) - 2.30258502 * jax.random.uniform(arg_keys[3], (STRIPS, UNKNOWNS), jnp.float32) ** steps_of(arg_keys[3], (STRIPS, UNKNOWNS), ((0, 128),), -0.2, 0.2)), 0.001, 0.01),
        "col_blocks": different_ones(arg_keys[4], STRIPS, HARMONICS // 128, COL_BLOCKS, 0),
        "gravity": draw_gravity(jax.random.fold_in(arg_keys[6], 71), 0),
    }


HIGHEST = lax.Precision.HIGHEST

def batch_product(left, right):
    return jnp.einsum('sij,sjk->sik', left, right, precision=HIGHEST)

def flipped(matrix):
    return jnp.swapaxes(matrix, 1, 2)

def solve_many(matrix, rhs):

    def single(mat_one, rhs_one):
        return jax.scipy.linalg.cho_solve((jnp.linalg.cholesky(mat_one), True), rhs_one)
    return jax.vmap(single)(matrix, rhs)

def placement_table(col_blocks):
    offsets = jnp.arange(128, dtype=jnp.int32)
    target = (col_blocks[:, :, None] * 128 + offsets[None, None, :]).reshape(STRIPS, COUPLED)
    columns = jnp.arange(HARMONICS, dtype=jnp.int32)
    return (target[:, :, None] == columns[None, None, :]).astype(jnp.float32)

def reference(edge_map, couple_map, topo_rows, mass, col_blocks, gravity):
    identity = jnp.eye(UNKNOWNS, dtype=jnp.float32)
    weight = batch_product(flipped(edge_map), edge_map)
    behind = jnp.roll(weight, 1, axis=0)
    diag_block = weight + behind + batch_product(flipped(couple_map), couple_map) + mass[:, :, None] * identity
    upper_block = -weight
    lower_block = -behind
    table = placement_table(col_blocks)
    placed = batch_product(topo_rows, table)
    right_side = batch_product(flipped(couple_map), placed)
    for depth in range(LEVELS):
        stride = 2 ** depth
        solved_lower = solve_many(diag_block, lower_block)
        solved_upper = solve_many(diag_block, upper_block)
        solved_right = solve_many(diag_block, right_side)
        from_below = [jnp.roll(a, stride, axis=0) for a in (solved_lower, solved_upper, solved_right)]
        from_above = [jnp.roll(a, -stride, axis=0) for a in (solved_lower, solved_upper, solved_right)]
        new_lower = -batch_product(lower_block, from_below[0])
        new_upper = -batch_product(upper_block, from_above[1])
        diag_block = diag_block - batch_product(lower_block, from_below[1]) - batch_product(upper_block, from_above[0])
        right_side = right_side - batch_product(lower_block, from_below[2]) - batch_product(upper_block, from_above[2])
        lower_block, upper_block = (new_lower, new_upper)
    sensitivity = solve_many(diag_block + lower_block + upper_block, right_side)
    misfit = placed - batch_product(couple_map, sensitivity)
    local_term = batch_product(flipped(topo_rows), misfit)
    schur = gravity + jnp.einsum('skh,skj->hj', table, local_term, precision=HIGHEST)
    split_at = HARMONICS // 2
    corner = jnp.linalg.cholesky(schur[:split_at, :split_at])
    below = jax.scipy.linalg.solve_triangular(corner, schur[split_at:, :split_at].T, lower=True).T
    trailing = schur[split_at:, split_at:] - jnp.dot(below, below.T, precision=HIGHEST)
    top = jnp.concatenate([corner, jnp.zeros((split_at, HARMONICS - split_at), jnp.float32)], axis=1)
    bottom = jnp.concatenate([below, trailing], axis=1)
    factor = jnp.concatenate([top, bottom], axis=0)
    return (sensitivity, factor)
```

```python
import functools
import jax
import jax.numpy as jnp
from jax import lax
from jax.experimental import pallas as pl
from jax.experimental.pallas import tpu as pltpu
from jax.sharding import PartitionSpec as P

HIGHEST = lax.Precision.HIGHEST
F32 = jnp.float32
MESH = pl.DeviceIdType.MESH
N = 256
HALF = 512
NX, NYH, NZ, NC = 4, 2, 8, 2
VMEM = pltpu.VMEM


def dot(a, b):
    return lax.dot_general(a, b, (((1,), (0,)), ((), ())), precision=HIGHEST, preferred_element_type=F32)


def tdot(a, b):
    return lax.dot_general(a, b, (((0,), (0,)), ((), ())), precision=HIGHEST, preferred_element_type=F32)


def dott(a, b):
    return lax.dot_general(a, b, (((1,), (1,)), ((), ())), precision=HIGHEST, preferred_element_type=F32)


def eliminate(cols, rows, k0, nb, nl):
    nt = nb // 8
    row = lax.broadcasted_iota(jnp.int32, (8, 128), 0)
    lane = lax.broadcasted_iota(jnp.int32, (8, 128), 1)
    unit = [jnp.where(lane == (k0 % 128) + 8 * t + row, 1.0, 0.0).astype(F32) for t in range(nt)]
    pivots = []
    for k in range(nb):
        tk, r = k // 8, k % 8
        pivot = jnp.broadcast_to(cols[k][tk][r : r + 1, :], (8, 128))
        pivots.append(pivot)
        inverse = 1.0 / pivot
        mult = {}
        for t in range(tk, nt):
            if t > tk:
                mult[t] = cols[k][t] * inverse
            elif r < 7:
                mult[t] = jnp.where(row > r, cols[k][t] * inverse, 0.0)
        for j in range(k + 1, nb):
            tj = j // 8
            m = jnp.broadcast_to(mult[tj][j % 8 : j % 8 + 1, :], (8, 128))
            for t in range(tj, nt):
                cols[j][t] = cols[j][t] - cols[k][t] * m
        source = [jnp.broadcast_to(rows[tk][l][r : r + 1, :], (8, 128)) for l in range(nl)]
        unit_source = jnp.broadcast_to(unit[tk][r : r + 1, :], (8, 128))
        for t in mult:
            for l in range(nl):
                rows[t][l] = rows[t][l] - mult[t] * source[l]
            unit[t] = unit[t] - mult[t] * unit_source
    for t in range(nt):
        spread = pivots[8 * t]
        for r in range(1, 8):
            spread = jnp.where(row == r, pivots[8 * t + r], spread)
        scale = lax.rsqrt(spread)
        for l in range(nl):
            rows[t][l] = rows[t][l] * scale
        unit[t] = unit[t] * scale
    return rows, unit


def inverse_factor(mat, upper):
    nb, n = 32, N
    nt, nl = nb // 8, n // 128
    lane = lax.broadcasted_iota(jnp.int32, (8, 128), 1)
    for p in range(n // nb):
        k0 = p * nb
        k1 = k0 + nb
        ld, lo = k0 // 128, k0 % 128
        rows = [[mat[k0 + 8 * t : k0 + 8 * t + 8, 128 * l : 128 * l + 128] for l in range(nl)] for t in range(nt)]
        cols = [
            [None if t < j // 8 else jnp.broadcast_to(rows[t][ld][:, lo + j : lo + j + 1], (8, 128)) for t in range(nt)]
            for j in range(nb)
        ]
        rows, unit = eliminate(cols, rows, k0, nb, nl)
        inside = (lane >= lo) & (lane < lo + nb)
        for t in range(nt):
            for l in range(nl):
                upper[8 * t : 8 * t + 8, 128 * l : 128 * l + 128] = rows[t][l]
                value = jnp.where(inside, unit[t], rows[t][l]) if l == ld else rows[t][l]
                mat[k0 + 8 * t : k0 + 8 * t + 8, 128 * l : 128 * l + 128] = value
        if k1 < n:
            panel = mat[k0:k1, :]

            def update(a, b):
                at = lax.broadcasted_iota(jnp.int32, (b - a, n), 1)
                old = jnp.where((at >= k0) & (at < k1), 0.0, mat[a:b, :])
                mat[a:b, :] = old - tdot(upper[:, a:b], panel)

            update(k1, k1 + nb)
            if k1 + nb < n:
                update(k1 + nb, n)
        at = lax.broadcasted_iota(jnp.int32, (nb, n), 1)
        own = lax.broadcasted_iota(jnp.int32, (nb, n), 0) + k0
        mat[k0:k1, :] = jnp.where(at <= own, mat[k0:k1, :], 0.0)


def place_columns(compact, first, second, base, out):
    for b in range(HALF // 128):
        left = jnp.where(first == base + b, compact[:, :128], 0.0)
        right = jnp.where(second == base + b, compact[:, 128:], 0.0)
        out[:, 128 * b : 128 * b + 128] = left + right


def pre_kernel(edge, couple, topo, mass, weight, local, right):
    weight[...] = tdot(edge[...], edge[...])
    row = lax.broadcasted_iota(jnp.int32, (N, N), 0)
    col = lax.broadcasted_iota(jnp.int32, (N, N), 1)
    local[...] = tdot(couple[...], couple[...]) + jnp.where(row == col, mass[...], 0.0)
    right[...] = tdot(couple[...], topo[...])


def level0_kernel(blocks, weight, edge_behind, local, right, diag, ahead, back, right_ahead, right_back, mat, upper):
    base = lax.axis_index("harm") * 4
    behind = tdot(edge_behind[...], edge_behind[...])
    diag[...] = weight[...] + behind + local[...]
    mat[...] = diag[...]
    inverse_factor(mat, upper)
    inv = mat[...]
    low = -dot(inv, behind)
    up = -dot(inv, weight[...])
    ahead[:N, :] = tdot(up, low)
    ahead[N:, :] = tdot(up, up)
    back[:N, :] = tdot(low, up)
    back[N:, :] = tdot(low, low)
    half = dot(inv, right[...])
    place_columns(tdot(up, half), blocks[0], blocks[1], base, right_ahead)
    place_columns(tdot(low, half), blocks[0], blocks[1], base, right_back)


def level1_kernel(diag, from_behind, from_ahead, diag_new, inv_out, low_out, up_out, ahead, back, upper):
    diag_new[...] = diag[...] - from_behind[N:, :] - from_ahead[N:, :]
    inv_out[...] = diag_new[...]
    inverse_factor(inv_out, upper)
    inv = inv_out[...]
    low = -dot(inv, from_behind[:N, :])
    up = -dot(inv, from_ahead[:N, :])
    low_out[...] = low
    up_out[...] = up
    cross = tdot(up, low)
    cross = 0.5 * (cross + cross.T)
    ahead[...] = tdot(up, up) + cross
    back[...] = tdot(low, low) + cross


def right1_kernel(blocks, right, from_behind, from_ahead, inv, low, up, right_new, right_ahead, right_back):
    base = lax.axis_index("harm") * 4
    place_columns(right[...], blocks[0], blocks[1], base, right_new)
    right_new[...] = right_new[...] - from_behind[...] - from_ahead[...]
    half = dot(inv[...], right_new[...])
    right_ahead[...] = tdot(up[...], half)
    right_back[...] = tdot(low[...], half)


def last_kernel(diag, from_behind, from_ahead, inv_out, upper):
    inv_out[...] = diag[...] - from_behind[...] - from_ahead[...]
    inverse_factor(inv_out, upper)


def local_kernel(blocks, right, from_behind, from_ahead, inv, couple, topo, gravity, sens, top, bottom, misfit):
    base = lax.axis_index("harm") * 4
    strip = lax.axis_index("strip")
    total = right[...] - from_behind[...] - from_ahead[...]
    sens[...] = tdot(inv[...], dot(inv[...], total))
    place_columns(topo[...], blocks[0], blocks[1], base, misfit)
    term = tdot(topo[...], misfit[...] - dot(couple[...], sens[...]))
    for b in range(4):
        for shift, out in ((0, top), (4, bottom)):
            first = jnp.where(blocks[0] == b + shift, term[:128], 0.0)
            second = jnp.where(blocks[1] == b + shift, term[128:], 0.0)
            out[128 * b : 128 * b + 128, :] = first + second
    at = pl.multiple_of(8 * lax.rem(strip, 64), 8)

    @pl.when(strip < 64)
    def _():
        top[pl.ds(at, 8), :] += gravity[...]

    @pl.when(strip >= 64)
    def _():
        bottom[pl.ds(at, 8), :] += gravity[...]


def reduce_kernel(in0, in1, out0, out1, bc, wc, bx, wx, bz, wz, by, ssem, rsem):
    strip, harm = lax.axis_index("strip"), lax.axis_index("harm")
    c = lax.rem(strip, 2)
    z = lax.rem(strip // 2, NZ)
    yh = lax.rem(strip // 16, 2)
    x = strip // 32

    def at(x, yh, z, c):
        return (((x * 2 + yh) * NZ + z) * 2 + c, harm)

    core = at(x, yh, z, 1 - c)
    xs = [at(lax.rem(x + d, NX), yh, z, c) for d in range(1, NX)]
    zs = [at(x, yh, lax.rem(z + d, NZ), c) for d in range(1, NZ)]
    ys = at(x, 1 - yh, z, c)
    barrier = pltpu.get_barrier_semaphore()
    for peer in [core, ys] + xs + zs:
        pl.semaphore_signal(barrier, inc=1, device_id=peer, device_id_type=MESH)
    pl.semaphore_wait(barrier, 12)

    def send(src, dst, a, slot, peer):
        copy = pltpu.make_async_remote_copy(
            src_ref=src, dst_ref=dst, send_sem=ssem.at[a, slot], recv_sem=rsem.at[a, slot], device_id=peer, device_id_type=MESH
        )
        copy.start()
        return copy

    def aligned(v, m):
        return pl.multiple_of(v, m)

    ins, outs = (in0, in1), (out0, out1)
    pair = (0, 1)
    live = [
        [send(ins[a].at[:, pl.ds(aligned((1 - c) * 256, 256), 256)], bc.at[a], a, 0, core)] for a in pair
    ]

    def finish(a):
        for copy in live[a]:
            copy.wait()

    for a in pair:
        finish(a)
        wc[a] = ins[a][:, pl.ds(aligned(c * 256, 256), 256)] + bc[a]
        live[a] = [
            send(wc.at[a, pl.ds(aligned(lax.rem(x + d, NX) * 128, 128), 128)], bx.at[a, d - 1], a, d, xs[d - 1])
            for d in range(1, NX)
        ]
    for a in pair:
        finish(a)
        wx[a] = wc[a, pl.ds(aligned(x * 128, 128), 128)] + bx[a, 0] + bx[a, 1] + bx[a, 2]
        live[a] = [
            send(wx.at[a, pl.ds(aligned(lax.rem(z + d, NZ) * 16, 16), 16)], bz.at[a, d - 1], a, 3 + d, zs[d - 1])
            for d in range(1, NZ)
        ]
    for a in pair:
        finish(a)
        total = wx[a, pl.ds(aligned(z * 16, 16), 16)]
        for d in range(1, NZ):
            total = total + bz[a, d - 1]
        wz[a] = total
        live[a] = [send(wz.at[a, pl.ds(aligned((1 - yh) * 8, 8), 8)], by.at[a], a, 11, ys)]
    lanes = pl.ds(aligned(c * 256, 256), 256)
    row_x = x * 128
    row_z = row_x + z * 16
    row_y = row_z + yh * 8
    for a in pair:
        finish(a)
        piece = pl.ds(aligned(row_y, 8), 8)
        outs[a][piece, lanes] = wz[a, pl.ds(aligned(yh * 8, 8), 8)] + by[a]
        live[a] = [send(outs[a].at[piece, lanes], outs[a].at[piece, lanes], a, 12, ys)]
    for a in pair:
        finish(a)
        piece = pl.ds(aligned(row_z, 16), 16)
        live[a] = [
            send(outs[a].at[piece, lanes], outs[a].at[piece, lanes], a, 12 + d, zs[d - 1]) for d in range(1, NZ)
        ]
    for a in pair:
        finish(a)
        piece = pl.ds(aligned(row_x, 128), 128)
        live[a] = [
            send(outs[a].at[piece, lanes], outs[a].at[piece, lanes], a, 19 + d, xs[d - 1]) for d in range(1, NX)
        ]
    for a in pair:
        finish(a)
        live[a] = [send(outs[a].at[:, lanes], outs[a].at[:, lanes], a, 23, core)]
    for a in pair:
        finish(a)


def factor_kernel(corner, bottom, rows_out, update_out, sym, mat, inv, upper):
    strip = lax.axis_index("strip")
    sym[...] = 0.5 * (corner[...] + corner[...].T)
    mat[0] = sym[:N, :N]
    mat[1] = sym[N:, N:]

    def stage(i, carry):
        part = mat.at[i]
        inverse_factor(part, upper)

        @pl.when(i == 0)
        def _():
            inv[:N, N:] = dott(sym[N:, :N], part[...])
            mat[1] = mat[1] - dott(inv[:N, N:], inv[:N, N:])

        return carry

    lax.fori_loop(0, 2, stage, 0)
    inv[N:, :N] = -dot(mat[1], dot(inv[:N, N:], mat[0]))
    inv[:N, :N] = mat[0]
    inv[N:, N:] = mat[1]
    inv[:N, N:] = jnp.zeros((N, N), F32)
    row = pl.multiple_of(8 * lax.rem(strip, 64), 8)
    source = jnp.where(strip < 64, sym[pl.ds(row, 8), :], bottom[pl.ds(row, 8), :])
    solved = dott(source, inv[...])
    update_out[...] = dott(dot(solved, inv[...]), bottom[...])
    own = lax.broadcasted_iota(jnp.int32, (8, HALF), 0) + row
    col = lax.broadcasted_iota(jnp.int32, (8, HALF), 1)
    rows_out[...] = jnp.where((strip >= 64) | (col <= own), solved, 0.0)


def shape(*dims):
    return jax.ShapeDtypeStruct(dims, F32)


def call(body, outs, smem=0, ins=0, scratch=(), **params):
    full = pl.BlockSpec(memory_space=pltpu.VMEM)
    return pl.pallas_call(
        body,
        out_shape=outs,
        in_specs=[pl.BlockSpec(memory_space=pltpu.SMEM)] * smem + [full] * ins,
        out_specs=tuple(full for _ in outs),
        scratch_shapes=list(scratch),
        compiler_params=pltpu.CompilerParams(vmem_limit_bytes=48 << 20, **params),
    )


def shift(value, distance):
    size = lax.axis_size("strip")
    return lax.ppermute(value, "strip", [((i - distance) % size, i) for i in range(size)])


def shards(edge_map, couple_map, topo_rows, mass, col_blocks, gravity):
    edge, couple, topo, blocks = edge_map[0], couple_map[0], topo_rows[0], col_blocks[0]
    strip, harm = lax.axis_index("strip"), lax.axis_index("harm")
    upper = VMEM((32, N), F32)
    mat = VMEM((N, N), F32)
    sq, tall, wide, big = shape(N, N), shape(2 * N, N), shape(N, HALF), shape(HALF, HALF)
    edge_behind = shift(edge, 1)
    weight, local, right = call(pre_kernel, (sq, sq, sq), 0, 4)(edge, couple, topo, mass)
    diag, ahead, back, right_ahead, right_back = call(
        level0_kernel, (sq, tall, tall, wide, wide), 1, 4, (mat, upper)
    )(blocks, weight, edge_behind, local, right)
    behind, front = shift(ahead, 1), shift(back, -1)
    right_behind, right_front = shift(right_ahead, 1), shift(right_back, -1)
    diag, inv, low, up, ahead, back = call(level1_kernel, (sq,) * 6, 0, 3, (upper,))(diag, behind, front)
    behind, front = shift(ahead, 2), shift(back, -2)
    right, right_ahead, right_back = call(right1_kernel, (wide, wide, wide), 1, 6)(
        blocks, right, right_behind, right_front, inv, low, up
    )
    right_behind, right_front = shift(right_ahead, 2), shift(right_back, -2)
    (inv,) = call(last_kernel, (sq,), 0, 3, (upper,))(diag, behind, front)
    sens, top, bottom = call(local_kernel, (wide, big, big), 1, 7, (VMEM((N, HALF), F32),))(
        blocks, right, right_behind, right_front, inv, couple, topo, gravity
    )
    top, bottom = call(
        reduce_kernel,
        (big, big),
        0,
        2,
        (
            VMEM((2, HALF, N), F32),
            VMEM((2, HALF, N), F32),
            VMEM((2, 3, 128, N), F32),
            VMEM((2, 128, N), F32),
            VMEM((2, 7, 16, N), F32),
            VMEM((2, 16, N), F32),
            VMEM((2, 8, N), F32),
            pltpu.SemaphoreType.DMA((2, 24)),
            pltpu.SemaphoreType.DMA((2, 24)),
        ),
        collective_id=0,
        has_side_effects=True,
    )(top, bottom)
    rows, update = call(
        factor_kernel,
        (shape(8, HALF), shape(8, HALF)),
        0,
        2,
        (VMEM((HALF, HALF), F32), VMEM((2, N, N), F32), VMEM((HALF, HALF), F32), upper),
    )(top, bottom)
    update = lax.ppermute(update, "harm", [(0, 1)])
    own = lax.dynamic_slice_in_dim(bottom, 8 * (strip % 64), 8, 0)
    trailing = jnp.where(strip < 64, 0.0, own - update)
    return sens[None], jnp.where(harm == 0, rows, trailing)


def solution(mesh):
    placed = (
        P("strip", None, None),
        P("strip", None, None),
        P("strip", None, None),
        P("strip", None),
        P("strip", None),
        P("strip", "harm"),
    )
    return jax.shard_map(
        shards,
        mesh=mesh,
        in_specs=placed,
        out_specs=(P("strip", None, "harm"), P("strip", "harm")),
        check_vma=False,
    )
```

```python
import functools
import jax
import jax.numpy as jnp
from jax import lax
from jax.experimental import pallas as pl
from jax.experimental.pallas import tpu as pltpu
from jax.sharding import PartitionSpec as P

HIGHEST = lax.Precision.HIGHEST
F32 = jnp.float32
MESH = pl.DeviceIdType.MESH
N = 256
HALF = 512
NX, NYH, NZ, NC = 4, 2, 8, 2
VMEM = pltpu.VMEM


def dot(a, b):
    return lax.dot_general(a, b, (((1,), (0,)), ((), ())), precision=HIGHEST, preferred_element_type=F32)


def tdot(a, b):
    return lax.dot_general(a, b, (((0,), (0,)), ((), ())), precision=HIGHEST, preferred_element_type=F32)


def dott(a, b):
    return lax.dot_general(a, b, (((1,), (1,)), ((), ())), precision=HIGHEST, preferred_element_type=F32)


def eliminate(cols, rows, lo, nb):
    iota = lax.broadcasted_iota(jnp.int32, (nb, 128), 0)
    lane = lax.broadcasted_iota(jnp.int32, (nb, 128), 1)
    work = [rows, jnp.where(lane == lo + iota, 1.0, 0.0).astype(F32)]
    done = [[], []]
    pivots = []
    for k in range(nb):
        r = k % 8
        n = nb - 8 * (k // 8)
        pivot = jnp.broadcast_to(cols[k][r : r + 1, :], (n, 128))
        pivots.append(pivot[:8])
        mult = jnp.where(iota[:n] > r, cols[k] * (1.0 / pivot), 0.0)
        for j in range(k + 1, nb):
            at = 8 * (j // 8) - 8 * (k // 8)
            own = j - 8 * (k // 8)
            m = jnp.broadcast_to(mult[own : own + 1, :], (n - at, 128))
            cols[j] = cols[j] - cols[k][at:] * m
        for i in range(2):
            work[i] = work[i] - mult * jnp.broadcast_to(work[i][r : r + 1, :], (n, 128))
            if r == 7:
                done[i].append(work[i][:8])
                work[i] = work[i][8:]
    scales = []
    for t in range(nb // 8):
        spread = pivots[8 * t]
        for r in range(1, 8):
            spread = jnp.where(iota[:8] == r, pivots[8 * t + r], spread)
        scales.append(lax.rsqrt(spread))
    scale = jnp.concatenate(scales, 0)
    return jnp.concatenate(done[0], 0) * scale, jnp.concatenate(done[1], 0) * scale


def small_inverse(mat):
    nb, n = 32, 128
    lane = lax.broadcasted_iota(jnp.int32, (nb, n), 1)
    own = lax.broadcasted_iota(jnp.int32, (nb, n), 0)
    for p in range(n // nb):
        k0 = p * nb
        k1 = k0 + nb
        rows = mat[k0:k1, :]
        cols = [
            jnp.broadcast_to(rows[8 * (j // 8) :, k0 + j : k0 + j + 1], (nb - 8 * (j // 8), n)) for j in range(nb)
        ]
        up, unit = eliminate(cols, rows, k0, nb)
        panel = jnp.where((lane >= k0) & (lane < k1), unit, up)

        def update(a, b):
            at = lax.broadcasted_iota(jnp.int32, (b - a, n), 1)
            old = jnp.where((at >= k0) & (at < k1), 0.0, mat[a:b, :])
            mat[a:b, :] = old - tdot(up[:, a:b], panel)

        if k1 < n:
            update(k1, k1 + nb)
        if k1 + nb < n:
            update(k1 + nb, n)
        mat[k0:k1, :] = jnp.where(lane <= own + k0, panel, 0.0)


def inverse_factor(mat, pair):
    pair[0] = mat[:128, :128]

    def stage(i, carry):
        part = pair.at[i]
        small_inverse(part)

        @pl.when(i == 0)
        def _():
            low = dott(mat[128:, :128], part[...])
            mat[128:, :128] = low
            pair[1] = mat[128:, 128:] - dott(low, low)

        return carry

    lax.fori_loop(0, 2, stage, 0)
    mat[128:, :128] = -dot(pair[1], dot(mat[128:, :128], pair[0]))
    mat[:128, :128] = pair[0]
    mat[128:, 128:] = pair[1]
    mat[:128, 128:] = jnp.zeros((128, 128), F32)


def place_columns(compact, ids, first, second):
    left = jnp.where(ids == first, jnp.concatenate([compact[:, :128]] * 4, 1), 0.0)
    return left + jnp.where(ids == second, jnp.concatenate([compact[:, 128:]] * 4, 1), 0.0)


def whole_kernel(
    blocks, mass, edge_in, couple_in, topo_in, gravity, sens, out,
    edge, edge_behind, couple, topo, weight, diag, right_c, mat, low, up, pair,
    ahead, back, behind, front, right, right_ahead, right_back, right_behind, right_front,
    bc, wc, bx, wx, bz, wz, by, half0, half1, full0, full1, sym, corner, inv, update, remote,
    local_sem, nsend, nrecv, ssem, rsem,
):
    strip, harm = lax.axis_index("strip"), lax.axis_index("harm")
    c = lax.rem(strip, 2)
    z = lax.rem(strip // 2, NZ)
    yh = lax.rem(strip // 16, 2)
    x = strip // 32
    strips = NX * NYH * NZ * NC

    def at(x, yh, z, c):
        return (((x * 2 + yh) * NZ + z) * 2 + c, harm)

    def along(distance):
        return (lax.rem(strip + distance + strips, strips), harm)

    core = at(x, yh, z, 1 - c)
    xs = [at(lax.rem(x + d, NX), yh, z, c) for d in range(1, NX)]
    zs = [at(x, yh, lax.rem(z + d, NZ), c) for d in range(1, NZ)]
    ys = at(x, 1 - yh, z, c)
    mirror = (strip, 1 - harm)
    barrier = pltpu.get_barrier_semaphore()
    peers = [along(1), along(-1), along(2), along(-2), core, ys, mirror] + xs + zs
    for peer in peers:
        pl.semaphore_signal(barrier, inc=1, device_id=peer, device_id_type=MESH)
    loads = [
        pltpu.make_async_copy(src.at[0], dst, local_sem.at[i])
        for i, (src, dst) in enumerate(((edge_in, edge), (couple_in, couple), (topo_in, topo)))
    ]
    for load in loads:
        load.start()
    for load in loads:
        load.wait()

    def push(src, dst, slot, peer):
        copy = pltpu.make_async_remote_copy(
            src_ref=src, dst_ref=dst, send_sem=nsend.at[slot], recv_sem=nrecv.at[slot], device_id=peer, device_id_type=MESH
        )
        copy.start()
        return copy

    weight[...] = tdot(edge[...], edge[...])
    row = lax.broadcasted_iota(jnp.int32, (N, N), 0)
    col = lax.broadcasted_iota(jnp.int32, (N, N), 1)
    diag[...] = weight[...] + tdot(couple[...], couple[...]) + jnp.where(row == col, mass[...], 0.0)
    right_c[...] = tdot(couple[...], topo[...])
    pl.semaphore_wait(barrier, len(peers))
    move = push(edge, edge_behind, 0, along(1))
    ids = lax.broadcasted_iota(jnp.int32, (N, HALF), 1) // 128 + harm * 4
    first, second = blocks[0, 0], blocks[0, 1]
    right[...] = place_columns(right_c[...], ids, first, second)
    move.wait()

    lower = tdot(edge_behind[...], edge_behind[...])
    diag[...] = diag[...] + lower
    mat[...] = diag[...]
    edge_behind[...] = lower
    inverse_factor(mat, pair)
    low[...] = -dot(mat[...], edge_behind[...])
    up[...] = -dot(mat[...], weight[...])
    ahead[0] = tdot(up[...], low[...])
    ahead[1] = tdot(up[...], up[...])
    go_ahead = push(ahead.at[pl.ds(0, 2)], behind.at[pl.ds(0, 2)], 1, along(1))
    back[0] = tdot(low[...], up[...])
    back[1] = tdot(low[...], low[...])
    go_back = push(back.at[pl.ds(0, 2)], front.at[pl.ds(0, 2)], 2, along(-1))
    half = dot(mat[...], right_c[...])
    right_ahead[0] = place_columns(tdot(up[...], half), ids, first, second)
    right_go = push(right_ahead.at[0], right_behind.at[0], 3, along(1))
    right_back[0] = place_columns(tdot(low[...], half), ids, first, second)
    right_come = push(right_back.at[0], right_front.at[0], 4, along(-1))

    go_ahead.wait()
    go_back.wait()
    diag[...] = diag[...] - behind[1] - front[1]
    mat[...] = diag[...]
    inverse_factor(mat, pair)
    low[...] = -dot(mat[...], behind[0])
    up[...] = -dot(mat[...], front[0])
    cross = tdot(up[...], low[...])
    cross = 0.5 * (cross + cross.T)
    ahead[2] = tdot(up[...], up[...]) + cross
    go_ahead = push(ahead.at[2], behind.at[2], 5, along(2))
    back[2] = tdot(low[...], low[...]) + cross
    go_back = push(back.at[2], front.at[2], 6, along(-2))
    right_go.wait()
    right_come.wait()
    right[...] = right[...] - right_behind[0] - right_front[0]
    half = dot(mat[...], right[...])
    right_ahead[1] = tdot(up[...], half)
    right_go = push(right_ahead.at[1], right_behind.at[1], 7, along(2))
    right_back[1] = tdot(low[...], half)
    right_come = push(right_back.at[1], right_front.at[1], 8, along(-2))

    go_ahead.wait()
    go_back.wait()
    mat[...] = diag[...] - behind[2] - front[2]
    inverse_factor(mat, pair)
    right_go.wait()
    right_come.wait()
    right[...] = right[...] - right_behind[1] - right_front[1]
    sens[0] = tdot(mat[...], dot(mat[...], right[...]))
    right[...] = place_columns(topo[...], ids, first, second) - dot(couple[...], sens[0])
    right[...] = tdot(topo[...], right[...])
    for b in range(4):
        for shift, part in ((0, half0), (4, half1)):
            one = jnp.where(ids[:128] * 0 + first == b + shift, right[:128], 0.0)
            two = jnp.where(ids[:128] * 0 + second == b + shift, right[128:], 0.0)
            part[128 * b : 128 * b + 128, :] = one + two
    mine = pl.ds(pl.multiple_of(8 * lax.rem(strip, 64), 8), 8)

    @pl.when(strip < 64)
    def _():
        half0[mine, :] += gravity[...]

    @pl.when(strip >= 64)
    def _():
        half1[mine, :] += gravity[...]

    ins, outs = (half0, half1), (full0, full1)
    lanes = pl.ds(pl.multiple_of(c * 256, 256), 256)
    row_x = x * 128
    row_z = row_x + z * 16
    row_y = row_z + yh * 8

    def send(a, src, dst, slot, peer):
        copy = pltpu.make_async_remote_copy(
            src_ref=src, dst_ref=dst, send_sem=ssem.at[a, slot], recv_sem=rsem.at[a, slot], device_id=peer, device_id_type=MESH
        )
        copy.start()
        return copy

    def finish(copies):
        for copy in copies:
            copy.wait()

    def sum_core(a):
        return [send(a, ins[a].at[:, pl.ds(pl.multiple_of((1 - c) * 256, 256), 256)], bc.at[a], 0, core)]

    def sum_x(a):
        wc[a] = ins[a][:, lanes] + bc[a]
        return [
            send(a, wc.at[a, pl.ds(pl.multiple_of(lax.rem(x + d, NX) * 128, 128), 128)], bx.at[a, d - 1], d, xs[d - 1])
            for d in range(1, NX)
        ]

    def sum_z(a):
        wx[a] = wc[a, pl.ds(pl.multiple_of(row_x, 128), 128)] + bx[a, 0] + bx[a, 1] + bx[a, 2]
        return [
            send(a, wx.at[a, pl.ds(pl.multiple_of(lax.rem(z + d, NZ) * 16, 16), 16)], bz.at[a, d - 1], 3 + d, zs[d - 1])
            for d in range(1, NZ)
        ]

    def sum_y(a):
        total = wx[a, pl.ds(pl.multiple_of(z * 16, 16), 16)]
        for d in range(1, NZ):
            total = total + bz[a, d - 1]
        wz[a] = total
        return [send(a, wz.at[a, pl.ds(pl.multiple_of((1 - yh) * 8, 8), 8)], by.at[a], 11, ys)]

    def spread(a, piece, slot, targets):
        view = outs[a].at[piece, lanes]
        return [send(a, view, view, slot + i, peer) for i, peer in enumerate(targets)]

    def spread_y(a):
        piece = pl.ds(pl.multiple_of(row_y, 8), 8)
        outs[a][piece, lanes] = wz[a, pl.ds(pl.multiple_of(yh * 8, 8), 8)] + by[a]
        return spread(a, piece, 12, [ys])

    def spread_z(a):
        return spread(a, pl.ds(pl.multiple_of(row_z, 16), 16), 13, zs)

    def spread_x(a):
        return spread(a, pl.ds(pl.multiple_of(row_x, 128), 128), 20, xs)

    def spread_core(a):
        return spread(a, slice(None), 23, [core])

    steps = (sum_core, sum_x, sum_z, sum_y, spread_y, spread_z, spread_x, spread_core)
    live = [[], []]

    def advance(a, s):
        finish(live[a])
        live[a] = steps[s](a) if s < len(steps) else []

    advance(0, 0)
    advance(0, 1)
    advance(1, 0)
    advance(0, 2)
    advance(1, 1)
    advance(0, 3)
    advance(0, 4)
    advance(0, 5)
    advance(1, 2)
    advance(0, 6)
    advance(1, 3)
    advance(0, 7)
    advance(1, 4)
    advance(0, 8)
    advance(1, 5)

    sym[...] = 0.5 * (full0[...] + full0[...].T)
    corner[0] = sym[:N, :N]
    corner[1] = sym[N:, N:]
    inverse_factor(corner.at[0], pair)
    advance(1, 6)
    inv[:N, N:] = dott(sym[N:, :N], corner[0])
    corner[1] = corner[1] - dott(inv[:N, N:], inv[:N, N:])
    inverse_factor(corner.at[1], pair)
    advance(1, 7)
    inv[N:, :N] = -dot(corner[1], dot(inv[:N, N:], corner[0]))
    inv[:N, :N] = corner[0]
    inv[N:, N:] = corner[1]
    inv[:N, N:] = jnp.zeros((N, N), F32)
    advance(1, 8)
    source = jnp.where(strip < 64, sym[mine, :], full1[mine, :])
    solved = dott(source, inv[...])
    update[...] = dott(dot(solved, inv[...]), full1[...])
    cross_over = push(update, remote, 9, mirror)
    at_row = lax.broadcasted_iota(jnp.int32, (8, HALF), 0) + 8 * lax.rem(strip, 64)
    at_col = lax.broadcasted_iota(jnp.int32, (8, HALF), 1)
    solved = jnp.where((strip >= 64) | (at_col <= at_row), solved, 0.0)
    own = full1[mine, :]
    cross_over.wait()
    trailing = jnp.where(strip < 64, 0.0, own - remote[...])
    out[...] = jnp.where(harm == 0, solved, trailing)


def shards(edge_map, couple_map, topo_rows, mass, col_blocks, gravity):
    vmem = pl.BlockSpec(memory_space=pltpu.VMEM)
    hbm = pl.BlockSpec(memory_space=pl.ANY)

    def v(*dims):
        return VMEM(dims, F32)

    scratch = [v(N, N)] * 2 + [v(N, N)] * 8 + [v(2, 128, 128)]
    scratch += [v(3, N, N)] * 4 + [v(N, HALF)] + [v(2, N, HALF)] * 4
    scratch += [v(2, HALF, N), v(2, HALF, N), v(2, 3, 128, N), v(2, 128, N), v(2, 7, 16, N), v(2, 16, N), v(2, 8, N)]
    scratch += [v(HALF, HALF)] * 4 + [v(HALF, HALF), v(2, N, N), v(HALF, HALF), v(8, HALF), v(8, HALF)]
    dma = pltpu.SemaphoreType.DMA
    scratch += [dma((3,)), dma((10,)), dma((10,)), dma((2, 24)), dma((2, 24))]
    return pl.pallas_call(
        whole_kernel,
        out_shape=(jax.ShapeDtypeStruct((1, N, HALF), F32), jax.ShapeDtypeStruct((8, HALF), F32)),
        in_specs=[pl.BlockSpec(memory_space=pltpu.SMEM), vmem, hbm, hbm, hbm, vmem],
        out_specs=(vmem, vmem),
        scratch_shapes=scratch,
        compiler_params=pltpu.CompilerParams(vmem_limit_bytes=60 << 20, collective_id=0, has_side_effects=True),
    )(col_blocks, mass, edge_map, couple_map, topo_rows, gravity)


def solution(mesh):
    placed = (
        P("strip", None, None),
        P("strip", None, None),
        P("strip", None, None),
        P("strip", None),
        P("strip", None),
        P("strip", "harm"),
    )
    return jax.shard_map(
        shards,
        mesh=mesh,
        in_specs=placed,
        out_specs=(P("strip", None, "harm"), P("strip", "harm")),
        check_vma=False,
    )
```

```python
import functools
import jax
import jax.numpy as jnp
from jax import lax
from jax.experimental import pallas as pl
from jax.experimental.pallas import tpu as pltpu
from jax.sharding import PartitionSpec as P

HIGHEST = lax.Precision.HIGHEST
F32 = jnp.float32
MESH = pl.DeviceIdType.MESH
N = 256
HALF = 512
NX, NYH, NZ, NC = 4, 2, 8, 2
VMEM = pltpu.VMEM


def dot(a, b):
    return lax.dot_general(a, b, (((1,), (0,)), ((), ())), precision=HIGHEST, preferred_element_type=F32)


def tdot(a, b):
    return lax.dot_general(a, b, (((0,), (0,)), ((), ())), precision=HIGHEST, preferred_element_type=F32)


def dott(a, b):
    return lax.dot_general(a, b, (((1,), (1,)), ((), ())), precision=HIGHEST, preferred_element_type=F32)


def eliminate(cols, rows, lo, nb):
    iota = lax.broadcasted_iota(jnp.int32, (nb, 128), 0)
    lane = lax.broadcasted_iota(jnp.int32, (nb, 128), 1)
    work = [rows, jnp.where(lane == lo + iota, 1.0, 0.0).astype(F32)]
    done = [[], []]
    pivots = []
    for k in range(nb):
        r = k % 8
        n = nb - 8 * (k // 8)
        pivot = jnp.broadcast_to(cols[k][r : r + 1, :], (n, 128))
        pivots.append(pivot[:8])
        mult = jnp.where(iota[:n] > r, cols[k] * (1.0 / pivot), 0.0)
        for j in range(k + 1, nb):
            at = 8 * (j // 8) - 8 * (k // 8)
            own = j - 8 * (k // 8)
            m = jnp.broadcast_to(mult[own : own + 1, :], (n - at, 128))
            cols[j] = cols[j] - cols[k][at:] * m
        for i in range(2):
            work[i] = work[i] - mult * jnp.broadcast_to(work[i][r : r + 1, :], (n, 128))
            if r == 7:
                done[i].append(work[i][:8])
                work[i] = work[i][8:]
    scales = []
    for t in range(nb // 8):
        spread = pivots[8 * t]
        for r in range(1, 8):
            spread = jnp.where(iota[:8] == r, pivots[8 * t + r], spread)
        scales.append(lax.rsqrt(spread))
    scale = jnp.concatenate(scales, 0)
    return jnp.concatenate(done[0], 0) * scale, jnp.concatenate(done[1], 0) * scale


def small_inverse(mat):
    nb, n = 32, 128
    lane = lax.broadcasted_iota(jnp.int32, (nb, n), 1)
    own = lax.broadcasted_iota(jnp.int32, (nb, n), 0)
    for p in range(n // nb):
        k0 = p * nb
        k1 = k0 + nb
        rows = mat[k0:k1, :]
        cols = [
            jnp.broadcast_to(rows[8 * (j // 8) :, k0 + j : k0 + j + 1], (nb - 8 * (j // 8), n)) for j in range(nb)
        ]
        up, unit = eliminate(cols, rows, k0, nb)
        panel = jnp.where((lane >= k0) & (lane < k1), unit, up)

        def update(a, b):
            at = lax.broadcasted_iota(jnp.int32, (b - a, n), 1)
            old = jnp.where((at >= k0) & (at < k1), 0.0, mat[a:b, :])
            mat[a:b, :] = old - tdot(up[:, a:b], panel)

        if k1 < n:
            update(k1, k1 + nb)
        if k1 + nb < n:
            update(k1 + nb, n)
        mat[k0:k1, :] = jnp.where(lane <= own + k0, panel, 0.0)


def inverse_factor(mat, pair, between=None):
    pair[0] = mat[:128, :128]

    def middle():
        low = dott(mat[128:, :128], pair[0])
        mat[128:, :128] = low
        pair[1] = mat[128:, 128:] - dott(low, low)

    def stage(i, carry):
        small_inverse(pair.at[i])
        pl.when(i == 0)(middle)
        return carry

    if between is None:
        lax.fori_loop(0, 2, stage, 0)
    else:
        small_inverse(pair.at[0])
        middle()
        between()
        small_inverse(pair.at[1])
    mat[128:, :128] = -dot(pair[1], dot(mat[128:, :128], pair[0]))
    mat[:128, :128] = pair[0]
    mat[128:, 128:] = pair[1]
    mat[:128, 128:] = jnp.zeros((128, 128), F32)


def place_columns(compact, ids, first, second):
    left = jnp.where(ids == first, jnp.concatenate([compact[:, :128]] * 4, 1), 0.0)
    return left + jnp.where(ids == second, jnp.concatenate([compact[:, 128:]] * 4, 1), 0.0)


def whole_kernel(
    blocks, mass, edge_in, couple_in, topo_in, gravity, sens, out,
    edge, edge_behind, couple, topo, weight, diag, right_c, mat, low, up, pair,
    ahead, back, behind, front, right, right_ahead, right_back, right_behind, right_front,
    half0, half1, cross01, sym, corner, inv, update, remote, local_sem, nsend, nrecv, *rest,
):
    strip, harm = lax.axis_index("strip"), lax.axis_index("harm")
    c = lax.rem(strip, 2)
    z = lax.rem(strip // 2, NZ)
    yh = lax.rem(strip // 16, 2)
    x = strip // 32
    strips = NX * NYH * NZ * NC

    def at(x, yh, z, c):
        return (((x * 2 + yh) * NZ + z) * 2 + c, harm)

    def along(distance):
        return (lax.rem(strip + distance + strips, strips), harm)

    core = at(x, yh, z, 1 - c)
    xs = [at(lax.rem(x + d, NX), yh, z, c) for d in range(1, NX)]
    zs = [at(x, yh, lax.rem(z + d, NZ), c) for d in range(1, NZ)]
    ys = at(x, 1 - yh, z, c)
    mirror = (strip, 1 - harm)
    barrier = pltpu.get_barrier_semaphore()
    peers = [along(1), along(-1), along(2), along(-2), core, ys, mirror] + xs + zs
    for peer in peers:
        pl.semaphore_signal(barrier, inc=1, device_id=peer, device_id_type=MESH)
    loads = [
        pltpu.make_async_copy(src.at[0], dst, local_sem.at[i])
        for i, (src, dst) in enumerate(((edge_in, edge), (couple_in, couple), (topo_in, topo)))
    ]
    for load in loads:
        load.start()
    for load in loads:
        load.wait()

    def push(src, dst, slot, peer):
        copy = pltpu.make_async_remote_copy(
            src_ref=src, dst_ref=dst, send_sem=nsend.at[slot], recv_sem=nrecv.at[slot], device_id=peer, device_id_type=MESH
        )
        copy.start()
        return copy

    lower_parts = ((slice(0, 128), slice(0, 128)), (slice(128, 256), slice(0, 256)))

    def push_lower(src, dst, slot, peer):
        return [push(src.at[rows, cols], dst.at[rows, cols], slot + i, peer) for i, (rows, cols) in enumerate(lower_parts)]

    def finish(copies):
        for copy in copies:
            copy.wait()

    weight[...] = tdot(edge[...], edge[...])
    row = lax.broadcasted_iota(jnp.int32, (N, N), 0)
    col = lax.broadcasted_iota(jnp.int32, (N, N), 1)
    diag[...] = weight[...] + tdot(couple[...], couple[...]) + jnp.where(row == col, mass[...], 0.0)
    right_c[...] = tdot(couple[...], topo[...])
    pl.semaphore_wait(barrier, len(peers))
    move = push(edge, edge_behind, 0, along(1))
    ids = lax.broadcasted_iota(jnp.int32, (N, HALF), 1) // 128 + harm * 4
    first, second = blocks[0, 0], blocks[0, 1]
    right[...] = place_columns(right_c[...], ids, first, second)
    move.wait()

    lower = tdot(edge_behind[...], edge_behind[...])
    diag[...] = diag[...] + lower
    mat[...] = diag[...]
    edge_behind[...] = lower
    inverse_factor(mat, pair)
    low[...] = -dot(mat[...], edge_behind[...])
    up[...] = -dot(mat[...], weight[...])
    ahead[0] = tdot(up[...], up[...])
    go_ahead = push_lower(ahead.at[0], behind.at[0], 1, along(1))
    back[0] = tdot(low[...], low[...])
    go_back = push_lower(back.at[0], front.at[0], 3, along(-1))
    ahead[1] = tdot(up[...], low[...])
    cross_ahead = push(ahead.at[1], behind.at[1], 5, along(1))
    back[1] = tdot(low[...], up[...])
    cross_back = push(back.at[1], front.at[1], 6, along(-1))
    half = dot(mat[...], right_c[...])
    right_ahead[0] = place_columns(tdot(up[...], half), ids, first, second)
    right_go = push(right_ahead.at[0], right_behind.at[0], 7, along(1))
    right_back[0] = place_columns(tdot(low[...], half), ids, first, second)
    right_come = push(right_back.at[0], right_front.at[0], 8, along(-1))

    finish(go_ahead + go_back)
    for rows, cols in lower_parts:
        diag[rows, cols] = diag[rows, cols] - behind[0, rows, cols] - front[0, rows, cols]
        mat[rows, cols] = diag[rows, cols]
    inverse_factor(mat, pair)
    cross_ahead.wait()
    cross_back.wait()
    low[...] = -dot(mat[...], behind[1])
    up[...] = -dot(mat[...], front[1])
    cross = tdot(up[...], low[...])
    cross = 0.5 * (cross + cross.T)
    ahead[2] = tdot(up[...], up[...]) + cross
    go_ahead = push_lower(ahead.at[2], behind.at[2], 9, along(2))
    back[2] = tdot(low[...], low[...]) + cross
    go_back = push_lower(back.at[2], front.at[2], 11, along(-2))
    right_go.wait()
    right_come.wait()
    right[...] = right[...] - right_behind[0] - right_front[0]
    half = dot(mat[...], right[...])
    right_ahead[1] = tdot(up[...], half)
    right_go = push(right_ahead.at[1], right_behind.at[1], 13, along(2))
    right_back[1] = tdot(low[...], half)
    right_come = push(right_back.at[1], right_front.at[1], 14, along(-2))

    finish(go_ahead + go_back)
    for rows, cols in lower_parts:
        mat[rows, cols] = diag[rows, cols] - behind[2, rows, cols] - front[2, rows, cols]
    inverse_factor(mat, pair)
    right_go.wait()
    right_come.wait()
    right[...] = right[...] - right_behind[1] - right_front[1]
    sens[0] = tdot(mat[...], dot(mat[...], right[...]))
    right[...] = place_columns(topo[...], ids, first, second) - dot(couple[...], sens[0])
    right[...] = tdot(topo[...], right[...])
    for b in range(4):
        for shift, part in ((0, half0), (4, half1)):
            one = jnp.where(ids[:128] * 0 + first == b + shift, right[:128], 0.0)
            two = jnp.where(ids[:128] * 0 + second == b + shift, right[128:], 0.0)
            part[128 * b : 128 * b + 128, :] = one + two
    mine = pl.ds(pl.multiple_of(8 * lax.rem(strip, 64), 8), 8)

    @pl.when(strip < 64)
    def _():
        half0[mine, :] += gravity[...]

    @pl.when(strip >= 64)
    def _():
        half1[mine, :] += gravity[...]

    cross01[...] = 0.5 * (half0[N:, :N] + half0[:N, N:].T)
    chunks = [half0.at[:N, :N], cross01, half0.at[N:, N:], half1.at[:, :N], half1.at[:, N:]]
    sizes = (N, N, N, HALF, HALF)
    spaces = [rest[8 * q : 8 * q + 8] for q in range(5)]
    ssem, rsem = rest[40], rest[41]
    mine_lanes = pl.ds(pl.multiple_of(c * 128, 128), 128)
    other_lanes = pl.ds(pl.multiple_of((1 - c) * 128, 128), 128)

    def send(q, src, dst, slot, peer):
        copy = pltpu.make_async_remote_copy(
            src_ref=src, dst_ref=dst, send_sem=ssem.at[q, slot], recv_sem=rsem.at[q, slot], device_id=peer, device_id_type=MESH
        )
        copy.start()
        return copy

    def block(index, size):
        return pl.ds(pl.multiple_of(index * size, size), size)

    def sum_core(q):
        bc = spaces[q][0]
        return [send(q, chunks[q].at[:, other_lanes], bc, 0, core)]

    def sum_x(q):
        bc, wc, bx = spaces[q][:3]
        size = sizes[q] // NX
        wc[...] = chunks[q][:, mine_lanes] + bc[...]
        return [
            send(q, wc.at[block(lax.rem(x + d, NX), size)], bx.at[d - 1], d, xs[d - 1]) for d in range(1, NX)
        ]

    def sum_z(q):
        wc, bx, wx, bz = spaces[q][1:5]
        size = sizes[q] // NX // NZ
        wx[...] = wc[block(x, sizes[q] // NX), :] + bx[0] + bx[1] + bx[2]
        return [
            send(q, wx.at[block(lax.rem(z + d, NZ), size)], bz.at[d - 1], 3 + d, zs[d - 1]) for d in range(1, NZ)
        ]

    def sum_y(q):
        wx, bz, wz, by = spaces[q][3:7]
        total = wx[block(z, sizes[q] // NX // NZ), :]
        for d in range(1, NZ):
            total = total + bz[d - 1]
        wz[...] = total
        return [send(q, wz, by, 11, ys)]

    def spread(q, piece, lanes, slot, targets):
        view = spaces[q][7].at[piece, lanes]
        return [send(q, view, view, slot + i, peer) for i, peer in enumerate(targets)]

    def spread_z(q):
        wz, by, full = spaces[q][5:8]
        piece = block(x * NZ + z, sizes[q] // NX // NZ)
        full[piece, mine_lanes] = wz[...] + by[...]
        return spread(q, piece, mine_lanes, 12, zs)

    def spread_x(q):
        return spread(q, block(x, sizes[q] // NX), mine_lanes, 19, xs)

    def spread_core(q):
        return spread(q, slice(None), mine_lanes, 22, [core])

    steps = (sum_core, sum_x, sum_z, sum_y, spread_z, spread_x, spread_core)
    live = [[], [], [], [], []]

    def tick(t):
        for q in range(5):
            s = t - q
            if 0 <= s <= len(steps):
                finish(live[q])
                live[q] = steps[s](q) if s < len(steps) else []

    for t in range(8):
        tick(t)

    full = [space[7] for space in spaces]
    sym[:N, :N] = 0.5 * (full[0][...] + full[0][...].T)
    sym[:N, N:] = jnp.zeros((N, N), F32)
    corner[0] = sym[:N, :N]
    inverse_factor(corner.at[0], pair, lambda: tick(8))
    tick(9)
    sym[N:, :N] = full[1][...]
    sym[N:, N:] = 0.5 * (full[2][...] + full[2][...].T)
    inv[:N, N:] = dott(sym[N:, :N], corner[0])
    corner[1] = sym[N:, N:] - dott(inv[:N, N:], inv[:N, N:])
    inverse_factor(corner.at[1], pair, lambda: tick(10))
    tick(11)
    inv[N:, :N] = -dot(corner[1], dot(inv[:N, N:], corner[0]))
    inv[:N, :N] = corner[0]
    inv[N:, N:] = corner[1]
    inv[:N, N:] = jnp.zeros((N, N), F32)
    bottom_rows = jnp.concatenate([full[3][mine, :], full[4][mine, :]], 1)
    source = jnp.where(strip < 64, sym[mine, :], bottom_rows)
    solved = dott(source, inv[...])
    back_solved = dot(solved, inv[...])
    update[...] = dott(back_solved[:, :N], full[3][...]) + dott(back_solved[:, N:], full[4][...])
    cross_over = push(update, remote, 15, mirror)
    at_row = lax.broadcasted_iota(jnp.int32, (8, HALF), 0) + 8 * lax.rem(strip, 64)
    at_col = lax.broadcasted_iota(jnp.int32, (8, HALF), 1)
    solved = jnp.where((strip >= 64) | (at_col <= at_row), solved, 0.0)
    cross_over.wait()
    trailing = jnp.where(strip < 64, 0.0, bottom_rows - remote[...])
    out[...] = jnp.where(harm == 0, solved, trailing)


def shards(edge_map, couple_map, topo_rows, mass, col_blocks, gravity):
    vmem = pl.BlockSpec(memory_space=pltpu.VMEM)
    hbm = pl.BlockSpec(memory_space=pl.ANY)

    def v(*dims):
        return VMEM(dims, F32)

    scratch = [v(N, N)] * 2 + [v(N, N)] * 8 + [v(2, 128, 128)]
    scratch += [v(3, N, N)] * 4 + [v(N, HALF)] + [v(2, N, HALF)] * 4
    dma = pltpu.SemaphoreType.DMA
    scratch += [v(HALF, HALF), v(HALF, HALF), v(N, N), v(HALF, HALF), v(2, N, N), v(HALF, HALF), v(8, HALF), v(8, HALF)]
    scratch += [dma((3,)), dma((16,)), dma((16,))]
    for n in (N, N, N, HALF, HALF):
        m, k = n // NX, n // NX // NZ
        scratch += [v(n, 128), v(n, 128), v(3, m, 128), v(m, 128), v(7, k, 128), v(k, 128), v(k, 128), v(n, N)]
    scratch += [dma((5, 23)), dma((5, 23))]
    return pl.pallas_call(
        whole_kernel,
        out_shape=(jax.ShapeDtypeStruct((1, N, HALF), F32), jax.ShapeDtypeStruct((8, HALF), F32)),
        in_specs=[pl.BlockSpec(memory_space=pltpu.SMEM), vmem, hbm, hbm, hbm, vmem],
        out_specs=(vmem, vmem),
        scratch_shapes=scratch,
        compiler_params=pltpu.CompilerParams(vmem_limit_bytes=60 << 20, collective_id=0, has_side_effects=True),
    )(col_blocks, mass, edge_map, couple_map, topo_rows, gravity)


def solution(mesh):
    placed = (
        P("strip", None, None),
        P("strip", None, None),
        P("strip", None, None),
        P("strip", None),
        P("strip", None),
        P("strip", "harm"),
    )
    return jax.shard_map(
        shards,
        mesh=mesh,
        in_specs=placed,
        out_specs=(P("strip", None, "harm"), P("strip", "harm")),
        check_vma=False,
    )
```

```python
import functools
import jax
import jax.numpy as jnp
from jax import lax
from jax.experimental import pallas as pl
from jax.experimental.pallas import tpu as pltpu
from jax.sharding import PartitionSpec as P

HIGHEST = lax.Precision.HIGHEST
F32 = jnp.float32
MESH = pl.DeviceIdType.MESH
N = 256
HALF = 512
NX, NYH, NZ, NC = 4, 2, 8, 2
VMEM = pltpu.VMEM


def dot(a, b):
    return lax.dot_general(a, b, (((1,), (0,)), ((), ())), precision=HIGHEST, preferred_element_type=F32)


def tdot(a, b):
    return lax.dot_general(a, b, (((0,), (0,)), ((), ())), precision=HIGHEST, preferred_element_type=F32)


def dott(a, b):
    return lax.dot_general(a, b, (((1,), (1,)), ((), ())), precision=HIGHEST, preferred_element_type=F32)


def eliminate(rows, lo, nb):
    group = 16
    iota = lax.broadcasted_iota(jnp.int32, (nb, 128), 0)
    lane = lax.broadcasted_iota(jnp.int32, (nb, 128), 1)
    work = [rows, jnp.where(lane == lo + iota, 1.0, 0.0).astype(F32)]
    done = [[], []]
    pivots = []
    cols = {}
    for k in range(nb):
        r, top = k % 8, 8 * (k // 8)
        n = nb - top
        end = k // group * group + group
        if k % group == 0:
            for j in range(k, end):
                at = 8 * (j // 8) - top
                cols[j] = jnp.broadcast_to(work[0][at:, lo + j : lo + j + 1], (n - at, 128))
            pivot = jnp.broadcast_to(cols[k][r : r + 1, :], (8, 128))
        pivots.append(pivot)
        inverse = 1.0 / pivot
        mult = cols[k] * (jnp.concatenate([inverse] * (n // 8), 0) if n > 8 else inverse)
        head = jnp.where(iota[:8] > r, mult[:8], 0.0)
        mult = jnp.concatenate([head, mult[8:]], 0) if n > 8 else head
        if k + 1 < end:
            own = k + 1 - top
            at = 8 * (own // 8)
            below = jnp.broadcast_to(cols[k + 1][own - at : own - at + 1, :], (8, 128))
            beside = jnp.broadcast_to(cols[k][own : own + 1, :], (8, 128))
            pivot = below - (beside * beside) * inverse
        for j in range(k + 1, end):
            own = j - top
            at = 8 * (own // 8)
            m = jnp.broadcast_to(mult[own : own + 1, :], (n - at, 128))
            cols[j] = cols[j] - cols[k][at:] * m
        for i in range(2):
            work[i] = work[i] - mult * jnp.broadcast_to(work[i][r : r + 1, :], (n, 128))
            if r == 7:
                done[i].append(work[i][:8])
                work[i] = work[i][8:]
    scales = []
    for t in range(nb // 8):
        spread = pivots[8 * t]
        for r in range(1, 8):
            spread = jnp.where(iota[:8] == r, pivots[8 * t + r], spread)
        scales.append(lax.rsqrt(spread))
    scale = jnp.concatenate(scales, 0)
    return jnp.concatenate(done[0], 0) * scale, jnp.concatenate(done[1], 0) * scale


def small_inverse(mat, between=None):
    nb = 64
    lane = lax.broadcasted_iota(jnp.int32, (nb, 128), 1)
    own = lax.broadcasted_iota(jnp.int32, (nb, 128), 0)
    up, unit = eliminate(mat[:nb, :], 0, nb)
    panel = jnp.where(lane < nb, unit, up)
    old = jnp.where(lane < nb, 0.0, mat[nb:, :])
    rest = old - tdot(up[:, nb:], panel)
    mat[:nb, :] = jnp.where(lane <= own, panel, 0.0)
    if between is not None:
        between()
    up, unit = eliminate(rest, nb, nb)
    panel = jnp.where(lane >= nb, unit, up)
    mat[nb:, :] = jnp.where(lane <= own + nb, panel, 0.0)


def inverse_factor(mat, pair, hooks=None):
    pair[0] = mat[:128, :128]

    def middle():
        low = dott(mat[128:, :128], pair[0])
        mat[128:, :128] = low
        pair[1] = mat[128:, 128:] - dott(low, low)

    def stage(i, carry):
        small_inverse(pair.at[i])
        pl.when(i == 0)(middle)
        return carry

    if hooks is None:
        lax.fori_loop(0, 2, stage, 0)
    else:
        small_inverse(pair.at[0], hooks[0])
        middle()
        hooks[1]()
        small_inverse(pair.at[1], hooks[2])
    mat[128:, :128] = -dot(pair[1], dot(mat[128:, :128], pair[0]))
    mat[:128, :128] = pair[0]
    mat[128:, 128:] = pair[1]
    mat[:128, 128:] = jnp.zeros((128, 128), F32)


def place_columns(compact, masks):
    left = jnp.where(masks[0], jnp.concatenate([compact[:, :128]] * 4, 1), 0.0)
    return left + jnp.where(masks[1], jnp.concatenate([compact[:, 128:]] * 4, 1), 0.0)


def whole_kernel(
    blocks, mass, edge_in, couple_in, topo_in, gravity, sens, out,
    edge, edge_behind, couple, topo, weight, diag, right_c, mat, low, up, pair,
    ahead, back, behind, front, right, right_ahead, right_back, right_behind, right_front,
    tags, tags_behind, tags_front, low_rows, low_rest, half0, half1, cross01, sym, corner, inv, update, remote, local_sem, nsend, nrecv, *rest,
):
    strip, harm = lax.axis_index("strip"), lax.axis_index("harm")
    c = lax.rem(strip, 2)
    z = lax.rem(strip // 2, NZ)
    yh = lax.rem(strip // 16, 2)
    x = strip // 32
    strips = NX * NYH * NZ * NC

    def at(x, yh, z, c):
        return (((x * 2 + yh) * NZ + z) * 2 + c, harm)

    def along(distance):
        return (lax.rem(strip + distance + strips, strips), harm)

    core = at(x, yh, z, 1 - c)
    xs = [at(lax.rem(x + d, NX), yh, z, c) for d in range(1, NX)]
    zs = [at(x, yh, lax.rem(z + d, NZ), c) for d in range(1, NZ)]
    ys = at(x, 1 - yh, z, c)
    mirror = (strip, 1 - harm)
    barrier = pltpu.get_barrier_semaphore()
    peers = [along(1), along(-1), along(2), along(-2), core, ys, mirror] + xs + zs
    for peer in peers:
        pl.semaphore_signal(barrier, inc=1, device_id=peer, device_id_type=MESH)
    loads = [
        pltpu.make_async_copy(src.at[0], dst, local_sem.at[i])
        for i, (src, dst) in enumerate(((edge_in, edge), (couple_in, couple), (topo_in, topo)))
    ]
    for load in loads:
        load.start()
    for load in loads:
        load.wait()

    def push(src, dst, slot, peer):
        copy = pltpu.make_async_remote_copy(
            src_ref=src, dst_ref=dst, send_sem=nsend.at[slot], recv_sem=nrecv.at[slot], device_id=peer, device_id_type=MESH
        )
        copy.start()
        return copy

    lower_parts = ((slice(0, 128), slice(0, 128)), (slice(128, 256), slice(0, 256)))

    def push_lower(src, dst, slot, peer):
        return [push(src.at[rows, cols], dst.at[rows, cols], slot + i, peer) for i, (rows, cols) in enumerate(lower_parts)]

    def finish(copies):
        for copy in copies:
            copy.wait()

    first, second = blocks[0, 0], blocks[0, 1]
    tag_row = lax.broadcasted_iota(jnp.int32, (8, HALF), 0)
    tags[...] = jnp.where(tag_row == 0, first, second).astype(F32)
    ids = (lax.broadcasted_iota(jnp.int32, (1, HALF), 1) // 128 + harm * 4).astype(F32)

    def masks_of(ref):
        return [jnp.broadcast_to(ref[i : i + 1, :] == ids, (N, HALF)) for i in range(2)]

    weight[...] = tdot(edge[...], edge[...])
    row = lax.broadcasted_iota(jnp.int32, (N, N), 0)
    col = lax.broadcasted_iota(jnp.int32, (N, N), 1)
    diag[...] = weight[...] + tdot(couple[...], couple[...]) + jnp.where(row == col, mass[...], 0.0)
    right_c[...] = tdot(couple[...], topo[...])
    pl.semaphore_wait(barrier, len(peers))
    move = push(edge, edge_behind, 0, along(1))
    tag_moves = [push(tags, tags_behind, 16, along(1)), push(tags, tags_front, 17, along(-1))]
    masks = masks_of(tags)
    right[...] = place_columns(right_c[...], masks)
    move.wait()

    lower = tdot(edge_behind[...], edge_behind[...])
    diag[...] = diag[...] + lower
    mat[...] = diag[...]
    edge_behind[...] = lower
    inverse_factor(mat, pair)
    low[...] = -dot(mat[...], edge_behind[...])
    up[...] = -dot(mat[...], weight[...])
    ahead[0] = tdot(up[...], up[...])
    go_ahead = push_lower(ahead.at[0], behind.at[0], 1, along(1))
    back[0] = tdot(low[...], low[...])
    go_back = push_lower(back.at[0], front.at[0], 3, along(-1))
    ahead[1] = tdot(up[...], low[...])
    cross_ahead = push(ahead.at[1], behind.at[1], 5, along(1))
    back[1] = tdot(low[...], up[...])
    cross_back = push(back.at[1], front.at[1], 6, along(-1))
    half = dot(mat[...], right_c[...])
    right_ahead[0, :, :N] = tdot(up[...], half)
    right_go = push(right_ahead.at[0, :, :N], right_behind.at[0, :, :N], 7, along(1))
    right_back[0, :, :N] = tdot(low[...], half)
    right_come = push(right_back.at[0, :, :N], right_front.at[0, :, :N], 8, along(-1))

    finish(go_ahead + go_back)
    for rows, cols in lower_parts:
        diag[rows, cols] = diag[rows, cols] - behind[0, rows, cols] - front[0, rows, cols]
        mat[rows, cols] = diag[rows, cols]
    inverse_factor(mat, pair)
    cross_ahead.wait()
    cross_back.wait()
    low[...] = -dot(mat[...], behind[1])
    up[...] = -dot(mat[...], front[1])
    cross = tdot(up[...], low[...])
    cross = 0.5 * (cross + cross.T)
    ahead[2] = tdot(up[...], up[...]) + cross
    go_ahead = push_lower(ahead.at[2], behind.at[2], 9, along(2))
    back[2] = tdot(low[...], low[...]) + cross
    go_back = push_lower(back.at[2], front.at[2], 11, along(-2))
    right_go.wait()
    right_come.wait()
    finish(tag_moves)
    for source, tag in ((right_behind, tags_behind), (right_front, tags_front)):
        right[...] = right[...] - place_columns(source[0, :, :N], masks_of(tag))
    half = dot(mat[...], right[...])
    right_ahead[1] = tdot(up[...], half)
    right_go = push(right_ahead.at[1], right_behind.at[1], 13, along(2))
    right_back[1] = tdot(low[...], half)
    right_come = push(right_back.at[1], right_front.at[1], 14, along(-2))

    finish(go_ahead + go_back)
    for rows, cols in lower_parts:
        mat[rows, cols] = diag[rows, cols] - behind[2, rows, cols] - front[2, rows, cols]
    inverse_factor(mat, pair)
    right_go.wait()
    right_come.wait()
    right[...] = right[...] - right_behind[1] - right_front[1]
    sens[0] = tdot(mat[...], dot(mat[...], right[...]))
    right[...] = place_columns(topo[...], masks_of(tags)) - dot(couple[...], sens[0])
    right[...] = tdot(topo[...], right[...])
    for b in range(4):
        for shift, part in ((0, half0), (4, half1)):
            block_id = jnp.float32(b + shift)
            one = jnp.where(jnp.broadcast_to(tags[0:1, :] == block_id, (128, HALF)), right[:128], 0.0)
            two = jnp.where(jnp.broadcast_to(tags[1:2, :] == block_id, (128, HALF)), right[128:], 0.0)
            part[128 * b : 128 * b + 128, :] = one + two
    mine = pl.ds(pl.multiple_of(8 * lax.rem(strip, 64), 8), 8)

    @pl.when(strip < 64)
    def _():
        half0[mine, :] += gravity[...]

    @pl.when(strip >= 64)
    def _():
        half1[mine, :] += gravity[...]

    cross01[:N, :] = 0.5 * (half0[N:, :N] + half0[:N, N:].T)
    cross01[N:, :] = half0[N:, N:]
    chunks = [half0.at[:N, :N], cross01, half1.at[:, :N], half1.at[:, N:]]
    sizes = (N, HALF, HALF, HALF)
    spaces = [rest[8 * q : 8 * q + 8] for q in range(4)]
    ssem, rsem = rest[32], rest[33]
    mine_lanes = pl.ds(pl.multiple_of(c * 128, 128), 128)
    other_lanes = pl.ds(pl.multiple_of((1 - c) * 128, 128), 128)

    def send(q, src, dst, slot, peer):
        copy = pltpu.make_async_remote_copy(
            src_ref=src, dst_ref=dst, send_sem=ssem.at[q, slot], recv_sem=rsem.at[q, slot], device_id=peer, device_id_type=MESH
        )
        copy.start()
        return copy

    def block(index, size):
        return pl.ds(pl.multiple_of(index * size, size), size)

    def sum_core(q):
        bc = spaces[q][0]
        return [send(q, chunks[q].at[:, other_lanes], bc, 0, core)]

    def sum_x(q):
        bc, wc, bx = spaces[q][:3]
        size = sizes[q] // NX
        wc[...] = chunks[q][:, mine_lanes] + bc[...]
        return [
            send(q, wc.at[block(lax.rem(x + d, NX), size)], bx.at[d - 1], d, xs[d - 1]) for d in range(1, NX)
        ]

    def sum_z(q):
        wc, bx, wx, bz = spaces[q][1:5]
        size = sizes[q] // NX // NZ
        wx[...] = wc[block(x, sizes[q] // NX), :] + bx[0] + bx[1] + bx[2]
        return [
            send(q, wx.at[block(lax.rem(z + d, NZ), size)], bz.at[d - 1], 3 + d, zs[d - 1]) for d in range(1, NZ)
        ]

    def sum_y(q):
        wx, bz, wz, by = spaces[q][3:7]
        total = wx[block(z, sizes[q] // NX // NZ), :]
        for d in range(1, NZ):
            total = total + bz[d - 1]
        wz[...] = total
        return [send(q, wz, by, 11, ys)]

    def spread(q, piece, lanes, slot, targets):
        view = spaces[q][7].at[piece, lanes]
        return [send(q, view, view, slot + i, peer) for i, peer in enumerate(targets)]

    def spread_z(q):
        wz, by, full = spaces[q][5:8]
        piece = block(x * NZ + z, sizes[q] // NX // NZ)
        full[piece, mine_lanes] = wz[...] + by[...]
        return spread(q, piece, mine_lanes, 12, zs)

    def spread_x(q):
        return spread(q, block(x, sizes[q] // NX), mine_lanes, 19, xs)

    def spread_core(q):
        return spread(q, slice(None), mine_lanes, 22, [core])

    steps = (sum_core, sum_x, sum_z, sum_y, spread_z, spread_x, spread_core)
    live = [[], [], [], []]

    def advance(q, s):
        finish(live[q])
        live[q] = steps[s](q) if s < len(steps) else []

    for t in range(6):
        for q in range(4):
            if t >= q:
                advance(q, t - q)
    advance(0, 6)
    advance(0, 7)

    full = [space[7] for space in spaces]
    sym[:N, :N] = 0.5 * (full[0][...] + full[0][...].T)
    corner[0] = sym[:N, :N]

    def hook_first():
        advance(1, 5)
        advance(2, 4)
        advance(3, 3)

    def hook_second():
        advance(1, 6)
        advance(2, 5)
        advance(3, 4)

    def nothing():
        pass

    inverse_factor(corner.at[0], pair, (hook_first, nothing, hook_second))
    advance(1, 7)
    inv[N:, :N] = dott(full[1][:N, :], corner[0])
    schur = 0.5 * (full[1][N:, :] + full[1][N:, :].T) - dott(inv[N:, :N], inv[N:, :N])
    inv[N:, N:] = schur
    corner[1] = schur

    def hook_third():
        advance(2, 6)
        advance(3, 5)

    def hook_fourth():
        advance(2, 7)
        low_rows[...] = dott(full[2][...], corner[0])

    def hook_last():
        advance(3, 6)

    inverse_factor(corner.at[1], pair, (hook_third, hook_fourth, hook_last))
    advance(3, 7)
    low_rest[...] = full[3][...] - dott(low_rows[...], inv[N:, :N])
    quarter = pl.ds(pl.multiple_of(8 * lax.rem(strip, 32), 8), 8)
    top_rows = dott(sym[quarter, :N], corner[0])
    upper_part, lower_part = strip < 32, strip < 64
    solved1 = jnp.where(
        upper_part, top_rows, jnp.where(lower_part, inv[pl.ds(pl.multiple_of(N + 8 * lax.rem(strip, 32), 8), 8), :N], low_rows[mine, :])
    )
    rest2 = jnp.where(lower_part, inv[pl.ds(pl.multiple_of(N + 8 * lax.rem(strip, 32), 8), 8), N:], low_rest[mine, :])
    solved2 = dott(rest2, corner[1])
    update[...] = dott(solved1, low_rows[...]) + dott(dot(solved2, corner[1]), low_rest[...])
    solved = jnp.concatenate([solved1, solved2], 1)
    bottom_rows = jnp.concatenate([full[2][mine, :], full[3][mine, :]], 1)
    cross_over = push(update, remote, 15, mirror)
    at_row = lax.broadcasted_iota(jnp.int32, (8, HALF), 0) + 8 * lax.rem(strip, 64)
    at_col = lax.broadcasted_iota(jnp.int32, (8, HALF), 1)
    solved = jnp.where((strip >= 64) | (at_col <= at_row), solved, 0.0)
    cross_over.wait()
    trailing = jnp.where(strip < 64, 0.0, bottom_rows - remote[...])
    out[...] = jnp.where(harm == 0, solved, trailing)


def shards(edge_map, couple_map, topo_rows, mass, col_blocks, gravity):
    vmem = pl.BlockSpec(memory_space=pltpu.VMEM)
    hbm = pl.BlockSpec(memory_space=pl.ANY)

    def v(*dims):
        return VMEM(dims, F32)

    scratch = [v(N, N)] * 2 + [v(N, N)] * 8 + [v(2, 128, 128)]
    scratch += [v(3, N, N)] * 4 + [v(N, HALF)] + [v(2, N, HALF)] * 4
    dma = pltpu.SemaphoreType.DMA
    scratch += [v(8, HALF)] * 3 + [v(HALF, N)] * 2
    scratch += [v(HALF, HALF), v(HALF, HALF), v(HALF, N), v(HALF, HALF), v(2, N, N), v(HALF, HALF), v(8, HALF), v(8, HALF)]
    scratch += [dma((3,)), dma((18,)), dma((18,))]
    for n in (N, HALF, HALF, HALF):
        m, k = n // NX, n // NX // NZ
        scratch += [v(n, 128), v(n, 128), v(3, m, 128), v(m, 128), v(7, k, 128), v(k, 128), v(k, 128), v(n, N)]
    scratch += [dma((4, 23)), dma((4, 23))]
    return pl.pallas_call(
        whole_kernel,
        out_shape=(jax.ShapeDtypeStruct((1, N, HALF), F32), jax.ShapeDtypeStruct((8, HALF), F32)),
        in_specs=[pl.BlockSpec(memory_space=pltpu.SMEM), vmem, hbm, hbm, hbm, vmem],
        out_specs=(vmem, vmem),
        scratch_shapes=scratch,
        compiler_params=pltpu.CompilerParams(vmem_limit_bytes=60 << 20, collective_id=0, has_side_effects=True),
    )(col_blocks, mass, edge_map, couple_map, topo_rows, gravity)


def solution(mesh):
    placed = (
        P("strip", None, None),
        P("strip", None, None),
        P("strip", None, None),
        P("strip", None),
        P("strip", None),
        P("strip", "harm"),
    )
    return jax.shard_map(
        shards,
        mesh=mesh,
        in_specs=placed,
        out_specs=(P("strip", None, "harm"), P("strip", "harm")),
        check_vma=False,
    )
```

```python
import functools
import jax
import jax.numpy as jnp
from jax import lax
from jax.experimental import pallas as pl
from jax.experimental.pallas import tpu as pltpu
from jax.sharding import PartitionSpec as P

HIGHEST = lax.Precision.HIGHEST
F32 = jnp.float32
MESH = pl.DeviceIdType.MESH
N = 256
HALF = 512
NX, NYH, NZ, NC = 4, 2, 8, 2
VMEM = pltpu.VMEM


def dot(a, b):
    return lax.dot_general(a, b, (((1,), (0,)), ((), ())), precision=HIGHEST, preferred_element_type=F32)


def tdot(a, b):
    return lax.dot_general(a, b, (((0,), (0,)), ((), ())), precision=HIGHEST, preferred_element_type=F32)


def dott(a, b):
    return lax.dot_general(a, b, (((1,), (1,)), ((), ())), precision=HIGHEST, preferred_element_type=F32)


def eliminate(rows, lo, nb, hooks):
    group = 16
    iota = lax.broadcasted_iota(jnp.int32, (nb, 128), 0)
    lane = lax.broadcasted_iota(jnp.int32, (nb, 128), 1)
    work = [rows, jnp.where(lane == lo + iota, 1.0, 0.0).astype(F32)]
    done = [[], []]
    pivots = []
    cols = {}
    for k in range(nb):
        r, top = k % 8, 8 * (k // 8)
        n = nb - top
        end = k // group * group + group
        if k % group == 0:
            hooks[k // group]()
            for j in range(k, end):
                at = 8 * (j // 8) - top
                cols[j] = jnp.broadcast_to(work[0][at:, lo + j : lo + j + 1], (n - at, 128))
            pivot = jnp.broadcast_to(cols[k][r : r + 1, :], (8, 128))
        pivots.append(pivot)
        inverse = 1.0 / pivot
        mult = cols[k] * (jnp.concatenate([inverse] * (n // 8), 0) if n > 8 else inverse)
        head = jnp.where(iota[:8] > r, mult[:8], 0.0)
        mult = jnp.concatenate([head, mult[8:]], 0) if n > 8 else head
        if k + 1 < end:
            own = k + 1 - top
            at = 8 * (own // 8)
            below = jnp.broadcast_to(cols[k + 1][own - at : own - at + 1, :], (8, 128))
            beside = jnp.broadcast_to(cols[k][own : own + 1, :], (8, 128))
            pivot = below - (beside * beside) * inverse
        for j in range(k + 1, end):
            own = j - top
            at = 8 * (own // 8)
            m = jnp.broadcast_to(mult[own : own + 1, :], (n - at, 128))
            cols[j] = cols[j] - cols[k][at:] * m
        for i in range(2):
            work[i] = work[i] - mult * jnp.broadcast_to(work[i][r : r + 1, :], (n, 128))
            if r == 7:
                done[i].append(work[i][:8])
                work[i] = work[i][8:]
    scales = []
    for t in range(nb // 8):
        spread = pivots[8 * t]
        for r in range(1, 8):
            spread = jnp.where(iota[:8] == r, pivots[8 * t + r], spread)
        scales.append(lax.rsqrt(spread))
    scale = jnp.concatenate(scales, 0)
    return jnp.concatenate(done[0], 0) * scale, jnp.concatenate(done[1], 0) * scale


def idle():
    pass


def small_inverse(mat, hooks=(idle,) * 8):
    nb = 64
    lane = lax.broadcasted_iota(jnp.int32, (nb, 128), 1)
    own = lax.broadcasted_iota(jnp.int32, (nb, 128), 0)
    up, unit = eliminate(mat[:nb, :], 0, nb, hooks[:4])
    panel = jnp.where(lane < nb, unit, up)
    old = jnp.where(lane < nb, 0.0, mat[nb:, :])
    rest = old - tdot(up[:, nb:], panel)
    mat[:nb, :] = jnp.where(lane <= own, panel, 0.0)
    up, unit = eliminate(rest, nb, nb, hooks[4:])
    panel = jnp.where(lane >= nb, unit, up)
    mat[nb:, :] = jnp.where(lane <= own + nb, panel, 0.0)


def inverse_factor(mat, pair, hooks=None):
    pair[0] = mat[:128, :128]

    def middle():
        low = dott(mat[128:, :128], pair[0])
        mat[128:, :128] = low
        pair[1] = mat[128:, 128:] - dott(low, low)

    def stage(i, carry):
        small_inverse(pair.at[i])
        pl.when(i == 0)(middle)
        return carry

    if hooks is None:
        lax.fori_loop(0, 2, stage, 0)
    else:
        small_inverse(pair.at[0], hooks[:8])
        middle()
        small_inverse(pair.at[1], hooks[8:])
    mat[128:, :128] = -dot(pair[1], dot(mat[128:, :128], pair[0]))
    mat[:128, :128] = pair[0]
    mat[128:, 128:] = pair[1]
    mat[:128, 128:] = jnp.zeros((128, 128), F32)


def place_columns(compact, masks):
    left = jnp.where(masks[0], jnp.concatenate([compact[:, :128]] * 4, 1), 0.0)
    return left + jnp.where(masks[1], jnp.concatenate([compact[:, 128:]] * 4, 1), 0.0)


def whole_kernel(
    blocks, mass, edge_in, couple_in, topo_in, gravity, sens_out, out,
    edge, behind_weight, couple, topo, weight, diag, right_c, mat, low, up, pair,
    ahead, back, behind, front, right, right_ahead, right_back, right_behind, right_front,
    sens, tags, tags_behind, tags_front, low_rows, low_rest, half0, half1, cross01, sym, corner, inv, update, remote, local_sem, nsend, nrecv, sens_sem, *rest,
):
    strip, harm = lax.axis_index("strip"), lax.axis_index("harm")
    c = lax.rem(strip, 2)
    z = lax.rem(strip // 2, NZ)
    yh = lax.rem(strip // 16, 2)
    x = strip // 32
    strips = NX * NYH * NZ * NC

    def at(x, yh, z, c):
        return (((x * 2 + yh) * NZ + z) * 2 + c, harm)

    def along(distance):
        return (lax.rem(strip + distance + strips, strips), harm)

    core = at(x, yh, z, 1 - c)
    xs = [at(lax.rem(x + d, NX), yh, z, c) for d in range(1, NX)]
    zs = [at(x, yh, lax.rem(z + d, NZ), c) for d in range(1, NZ)]
    os = [at(x, 1 - yh, lax.rem(z + d, NZ), c) for d in range(NZ)]
    mirror = (strip, 1 - harm)
    barrier = pltpu.get_barrier_semaphore()
    peers = [along(1), along(-1), along(2), along(-2), core, mirror] + xs + zs + os
    for peer in peers:
        pl.semaphore_signal(barrier, inc=1, device_id=peer, device_id_type=MESH)
    loads = [
        pltpu.make_async_copy(src.at[0], dst, local_sem.at[i])
        for i, (src, dst) in enumerate(((edge_in, edge), (couple_in, couple), (topo_in, topo)))
    ]
    for load in loads:
        load.start()
    for load in loads:
        load.wait()

    def push(src, dst, slot, peer):
        copy = pltpu.make_async_remote_copy(
            src_ref=src, dst_ref=dst, send_sem=nsend.at[slot], recv_sem=nrecv.at[slot], device_id=peer, device_id_type=MESH
        )
        copy.start()
        return copy

    lower_parts = ((slice(0, 128), slice(0, 128)), (slice(128, 256), slice(0, 256)))

    def push_lower(src, dst, slot, peer):
        return [push(src.at[rows, cols], dst.at[rows, cols], slot + i, peer) for i, (rows, cols) in enumerate(lower_parts)]

    def finish(copies):
        for copy in copies:
            copy.wait()

    first, second = blocks[0, 0], blocks[0, 1]
    tag_row = lax.broadcasted_iota(jnp.int32, (8, HALF), 0)
    tags[...] = jnp.where(tag_row == 0, first, second).astype(F32)
    ids = (lax.broadcasted_iota(jnp.int32, (1, HALF), 1) // 128 + harm * 4).astype(F32)

    def masks_of(ref):
        return [jnp.broadcast_to(ref[i : i + 1, :] == ids, (N, HALF)) for i in range(2)]

    weight[...] = tdot(edge[...], edge[...])
    row = lax.broadcasted_iota(jnp.int32, (N, N), 0)
    col = lax.broadcasted_iota(jnp.int32, (N, N), 1)
    diag[...] = weight[...] + tdot(couple[...], couple[...]) + jnp.where(row == col, mass[...], 0.0)
    right_c[...] = tdot(couple[...], topo[...])
    pl.semaphore_wait(barrier, len(peers))
    move = push_lower(weight, behind_weight, 18, along(1))
    tag_moves = [push(tags, tags_behind, 16, along(1)), push(tags, tags_front, 17, along(-1))]
    masks = masks_of(tags)
    right[...] = place_columns(right_c[...], masks)
    finish(move)

    behind_weight[:128, 128:] = behind_weight[128:, :128].T
    diag[...] = diag[...] + behind_weight[...]
    mat[...] = diag[...]
    inverse_factor(mat, pair)
    low[...] = -dot(mat[...], behind_weight[...])
    up[...] = -dot(mat[...], weight[...])
    ahead[0] = tdot(up[...], up[...])
    go_ahead = push_lower(ahead.at[0], behind.at[0], 1, along(1))
    back[0] = tdot(low[...], low[...])
    go_back = push_lower(back.at[0], front.at[0], 3, along(-1))
    ahead[1] = tdot(up[...], low[...])
    cross_ahead = push(ahead.at[1], behind.at[1], 5, along(1))
    back[1] = tdot(low[...], up[...])
    cross_back = push(back.at[1], front.at[1], 6, along(-1))
    half = dot(mat[...], right_c[...])
    right_ahead[0, :, :N] = tdot(up[...], half)
    right_go = push(right_ahead.at[0, :, :N], right_behind.at[0, :, :N], 7, along(1))
    right_back[0, :, :N] = tdot(low[...], half)
    right_come = push(right_back.at[0, :, :N], right_front.at[0, :, :N], 8, along(-1))

    finish(go_ahead + go_back)
    for rows, cols in lower_parts:
        diag[rows, cols] = diag[rows, cols] - behind[0, rows, cols] - front[0, rows, cols]
        mat[rows, cols] = diag[rows, cols]
    inverse_factor(mat, pair)
    cross_ahead.wait()
    cross_back.wait()
    low[...] = -dot(mat[...], behind[1])
    up[...] = -dot(mat[...], front[1])
    cross = tdot(up[...], low[...])
    cross = 0.5 * (cross + cross.T)
    ahead[2] = tdot(up[...], up[...]) + cross
    go_ahead = push_lower(ahead.at[2], behind.at[2], 9, along(2))
    back[2] = tdot(low[...], low[...]) + cross
    go_back = push_lower(back.at[2], front.at[2], 11, along(-2))
    right_go.wait()
    right_come.wait()
    finish(tag_moves)
    for source, tag in ((right_behind, tags_behind), (right_front, tags_front)):
        right[...] = right[...] - place_columns(source[0, :, :N], masks_of(tag))
    half = dot(mat[...], right[...])
    right_ahead[1] = tdot(up[...], half)
    right_go = push(right_ahead.at[1], right_behind.at[1], 13, along(2))
    right_back[1] = tdot(low[...], half)
    right_come = push(right_back.at[1], right_front.at[1], 14, along(-2))

    finish(go_ahead + go_back)
    for rows, cols in lower_parts:
        mat[rows, cols] = diag[rows, cols] - behind[2, rows, cols] - front[2, rows, cols]
    inverse_factor(mat, pair)
    right_go.wait()
    right_come.wait()
    right[...] = right[...] - right_behind[1] - right_front[1]
    sens[...] = tdot(mat[...], dot(mat[...], right[...]))
    right[...] = place_columns(topo[...], masks_of(tags)) - dot(couple[...], sens[...])
    sens_write = pltpu.make_async_copy(sens, sens_out.at[0], sens_sem)
    sens_write.start()
    right[...] = tdot(topo[...], right[...])
    for b in range(4):
        for shift, part in ((0, half0), (4, half1)):
            block_id = jnp.float32(b + shift)
            one = jnp.where(jnp.broadcast_to(tags[0:1, :] == block_id, (128, HALF)), right[:128], 0.0)
            two = jnp.where(jnp.broadcast_to(tags[1:2, :] == block_id, (128, HALF)), right[128:], 0.0)
            part[128 * b : 128 * b + 128, :] = one + two
    mine = pl.ds(pl.multiple_of(8 * lax.rem(strip, 64), 8), 8)

    @pl.when(strip < 64)
    def _():
        half0[mine, :] += gravity[...]

    @pl.when(strip >= 64)
    def _():
        half1[mine, :] += gravity[...]

    cross01[:N, :] = 0.5 * (half0[N:, :N] + half0[:N, N:].T)
    cross01[N:, :] = half0[N:, N:]
    chunks = [half0.at[:N, :N], cross01, half1.at[:, :N], half1.at[:, N:]]
    sizes = (N, HALF, HALF, HALF)
    spaces = [rest[8 * q : 8 * q + 8] for q in range(4)]
    ssem, rsem = rest[32], rest[33]
    mine_lanes = pl.ds(pl.multiple_of(c * 128, 128), 128)
    other_lanes = pl.ds(pl.multiple_of((1 - c) * 128, 128), 128)

    def send(q, src, dst, slot, peer):
        copy = pltpu.make_async_remote_copy(
            src_ref=src, dst_ref=dst, send_sem=ssem.at[q, slot], recv_sem=rsem.at[q, slot], device_id=peer, device_id_type=MESH
        )
        copy.start()
        return copy

    def block(index, size):
        return pl.ds(pl.multiple_of(index * size, size), size)

    def sum_core(q):
        bc = spaces[q][0]
        return [send(q, chunks[q].at[:, other_lanes], bc, 0, core)]

    def sum_x(q):
        bc, wc, bx = spaces[q][:3]
        size = sizes[q] // NX
        wc[...] = chunks[q][:, mine_lanes] + bc[...]
        return [
            send(q, wc.at[block(lax.rem(x + d, NX), size)], bx.at[d - 1], d, xs[d - 1]) for d in range(1, NX)
        ]

    def sum_z(q):
        wc, bx, wx, bz = spaces[q][1:5]
        size = sizes[q] // NX // NZ
        wx[...] = wc[block(x, sizes[q] // NX), :] + bx[0] + bx[1] + bx[2]
        return [
            send(q, wx.at[block(lax.rem(z + d, NZ), size)], bz.at[d - 1], 3 + d, zs[d - 1]) for d in range(1, NZ)
        ]

    def spread_plane(q):
        wx, bz, own, other = spaces[q][3:7]
        piece = block(z, sizes[q] // NX // NZ)
        total = wx[piece, :]
        for d in range(1, NZ):
            total = total + bz[d - 1]
        own[piece, :] = total
        here = [send(q, own.at[piece], own.at[piece], 11 + i, peer) for i, peer in enumerate(zs)]
        return here + [send(q, own.at[piece], other.at[piece], 18 + i, peer) for i, peer in enumerate(os)]

    def spread(q, piece, slot, targets):
        view = spaces[q][7].at[piece, mine_lanes]
        return [send(q, view, view, slot + i, peer) for i, peer in enumerate(targets)]

    def spread_x(q):
        own, other, full = spaces[q][5:8]
        piece = block(x, sizes[q] // NX)
        full[piece, mine_lanes] = own[...] + other[...]
        return spread(q, piece, 26, xs)

    def spread_core(q):
        return spread(q, slice(None), 29, [core])

    steps = (sum_core, sum_x, sum_z, spread_plane, spread_x, spread_core)
    live = [[], [], [], []]

    def advance(q, s):
        finish(live[q])
        live[q] = steps[s](q) if s < len(steps) else []

    advance(0, 0)
    advance(1, 0)
    advance(2, 0)
    advance(3, 0)
    advance(0, 1)
    advance(1, 1)
    advance(0, 2)
    advance(2, 1)
    advance(3, 1)
    advance(0, 3)
    advance(1, 2)
    advance(2, 2)
    advance(3, 2)
    advance(0, 4)
    advance(1, 3)
    advance(2, 3)
    advance(3, 3)
    advance(0, 5)
    advance(0, 6)

    full = [space[7] for space in spaces]
    sym[:N, :N] = 0.5 * (full[0][...] + full[0][...].T)
    corner[0] = sym[:N, :N]

    early = [idle] * 16

    def early_7():
        advance(1, 4)

    early[7] = early_7
    inverse_factor(corner.at[0], pair, early)
    advance(1, 5)
    advance(2, 4)
    advance(3, 4)
    advance(1, 6)
    inv[N:, :N] = dott(full[1][:N, :], corner[0])
    schur = 0.5 * (full[1][N:, :] + full[1][N:, :].T) - dott(inv[N:, :N], inv[N:, :N])
    inv[N:, N:] = schur
    corner[1] = schur

    late = [idle] * 16

    def late_10():
        advance(2, 5)
        advance(3, 5)

    late[10] = late_10

    def late_15():
        advance(2, 6)
        advance(3, 6)
        low_rows[...] = dott(full[2][...], corner[0])
        low_rest[...] = full[3][...] - dott(low_rows[...], inv[N:, :N])

    late[15] = late_15
    inverse_factor(corner.at[1], pair, late)
    quarter = pl.ds(pl.multiple_of(8 * lax.rem(strip, 32), 8), 8)
    top_rows = dott(sym[quarter, :N], corner[0])
    upper_part, lower_part = strip < 32, strip < 64
    solved1 = jnp.where(
        upper_part, top_rows, jnp.where(lower_part, inv[pl.ds(pl.multiple_of(N + 8 * lax.rem(strip, 32), 8), 8), :N], low_rows[mine, :])
    )
    rest2 = jnp.where(lower_part, inv[pl.ds(pl.multiple_of(N + 8 * lax.rem(strip, 32), 8), 8), N:], low_rest[mine, :])
    solved2 = dott(rest2, corner[1])
    update[...] = dott(solved1, low_rows[...]) + dott(dot(solved2, corner[1]), low_rest[...])
    solved = jnp.concatenate([solved1, solved2], 1)
    bottom_rows = jnp.concatenate([full[2][mine, :], full[3][mine, :]], 1)
    cross_over = push(update, remote, 15, mirror)
    at_row = lax.broadcasted_iota(jnp.int32, (8, HALF), 0) + 8 * lax.rem(strip, 64)
    at_col = lax.broadcasted_iota(jnp.int32, (8, HALF), 1)
    solved = jnp.where((strip >= 64) | (at_col <= at_row), solved, 0.0)
    cross_over.wait()
    sens_write.wait()
    trailing = jnp.where(strip < 64, 0.0, bottom_rows - remote[...])
    out[...] = jnp.where(harm == 0, solved, trailing)


def shards(edge_map, couple_map, topo_rows, mass, col_blocks, gravity):
    vmem = pl.BlockSpec(memory_space=pltpu.VMEM)
    hbm = pl.BlockSpec(memory_space=pl.ANY)

    def v(*dims):
        return VMEM(dims, F32)

    scratch = [v(N, N)] * 2 + [v(N, N)] * 8 + [v(2, 128, 128)]
    scratch += [v(3, N, N)] * 4 + [v(N, HALF)] + [v(2, N, HALF)] * 4
    dma = pltpu.SemaphoreType.DMA
    scratch += [v(N, HALF)] + [v(8, HALF)] * 3 + [v(HALF, N)] * 2
    scratch += [v(HALF, HALF), v(HALF, HALF), v(HALF, N), v(HALF, HALF), v(2, N, N), v(HALF, HALF), v(8, HALF), v(8, HALF)]
    scratch += [dma((3,)), dma((20,)), dma((20,)), dma]
    for n in (N, HALF, HALF, HALF):
        m, k = n // NX, n // NX // NZ
        scratch += [v(n, 128), v(n, 128), v(3, m, 128), v(m, 128), v(7, k, 128), v(m, 128), v(m, 128), v(n, N)]
    scratch += [dma((4, 30)), dma((4, 30))]
    return pl.pallas_call(
        whole_kernel,
        out_shape=(jax.ShapeDtypeStruct((1, N, HALF), F32), jax.ShapeDtypeStruct((8, HALF), F32)),
        in_specs=[pl.BlockSpec(memory_space=pltpu.SMEM), vmem, hbm, hbm, hbm, vmem],
        out_specs=(hbm, vmem),
        scratch_shapes=scratch,
        compiler_params=pltpu.CompilerParams(vmem_limit_bytes=60 << 20, collective_id=0, has_side_effects=True),
    )(col_blocks, mass, edge_map, couple_map, topo_rows, gravity)


def solution(mesh):
    placed = (
        P("strip", None, None),
        P("strip", None, None),
        P("strip", None, None),
        P("strip", None),
        P("strip", None),
        P("strip", "harm"),
    )
    return jax.shard_map(
        shards,
        mesh=mesh,
        in_specs=placed,
        out_specs=(P("strip", None, "harm"), P("strip", "harm")),
        check_vma=False,
    )
```
